32 devices in a mesh: mem: 8 (over z, y), tile: 4 (over x, core).
Axes of the slice: x: 2, y: 2, z: 4, core: 2. Of those that a mesh axis runs over, the one named last changes fastest.
Arguments:
- initial_realization_fields: float32 [128, 3, 4, 32, 128], P('mem', None, None, 'tile'), may hold values from -6 to 6, as said below
- measurement_location_offset: int32 [1024], replicated, may hold values from 0 to 32767
- observed: float32 [1024], P('tile'), may hold values from -6 to 6
- obs_var: float32 [1024], P('tile'), may hold values from 0.25 to 4
- obs_noise: float32 [1024, 128], P('tile', 'mem'), may hold values from -6 to 6
Outputs:
- analysis: float32 [128, 3, 4, 32, 128], P('mem', None, None, 'tile')
The draws below stay inside these ranges and needn't reach their ends.
Inputs may be any that keep to these rules, and one draw needn't show every extreme that they name: `initial_realization_fields`: field 0 of each member is the log-conductivity, field 1 the head, field 2 the salinity.
All inputs are finite; a program needn't handle non-finite values.
Results may differ from the reference program's by a relative error of at most 0.000076.
Values sent between devices are 32-bit elements; how exact they have to be, the bound alone decides.
A program may use at most 64 MiB of HBM per device.

```python
import math
import jax
import jax.numpy as jnp
from jax import lax

NE = 128
NZ = 4
NY = 128
NX = 32
ND = 1024


def draw_initial_realization_fields(key, part):
    grid_shape = (NE, NZ, NX, NY)
    key_cond, key_head, key_salt = jax.random.split(key, 3)
    log_cond = 0.35 * jnp.clip(jax.random.normal(key_cond, grid_shape, jnp.float32), -6.0, 6.0)
    head_now = jnp.clip(jax.random.normal(key_head, grid_shape, jnp.float32), -6.0, 6.0)
    salt_now = jax.random.uniform(key_salt, grid_shape, jnp.float32, 0.0, 1.0)
    return jnp.stack([log_cond, head_now, salt_now], axis=1)


def with_ends(entries, rng, least, largest):
    index_at = [jax.random.randint(jax.random.fold_in(rng, axis), (), 0, length) for axis, length in enumerate(entries.shape)]
    longest = entries.shape.index(max(entries.shape))
    beside = index_at[:longest] + [(index_at[longest] + 1) % entries.shape[longest]] + index_at[longest + 1:]
    return entries.at[tuple(index_at)].set(least).at[tuple(beside)].set(largest)


def shard_levels(stream_key, extent, pieces, least, high):
    level = 1.0
    for dim, blocks in pieces:
        draws = jax.random.uniform(jax.random.fold_in(jax.random.fold_in(stream_key, 6), dim), (blocks,), jnp.float32, least / len(pieces), high / len(pieces))
        level = level * jnp.repeat(jnp.exp(draws), extent[dim] // blocks).reshape((-1,) + (1,) * (len(extent) - 1 - dim))
    return level


def centred(key, shape, scale, most, pieces=(), kind=jnp.bfloat16):
    entries = scale * jax.random.normal(key, shape, jnp.float32)
    if pieces:
        entries = entries * shard_levels(key, shape, pieces, -0.22, 0.18)
    return jnp.clip(entries, -most, most).astype(kind)


def setup_inputs(seed: int = 0) -> dict:
    key_list = jax.random.split(jax.random.key(seed), 6)
    initial_realization_fields = draw_initial_realization_fields(jax.random.fold_in(key_list[5], 71), 0)
    measurement_location_offset = with_ends(jax.random.randint(key_list[1], (ND,), 0, 2 * NZ * NX * NY), jax.random.fold_in(key_list[1], 1), 0, (2 * NZ * NX * NY) - 1).astype(jnp.int32)
    observed = centred(key_list[2], (ND,), 1.0, 6.0, ((0, 4),), jnp.float32)
    obs_var = jnp.clip(jnp.exp(math.log(4.0) - 2.7725887 * jax.random.uniform(key_list[3], (ND,), jnp.float32) ** shard_levels(key_list[3], (ND,), ((0, 4),), -0.2, 0.2)), 0.25, 4.0)
    obs_noise = centred(key_list[4], (ND, NE), 1.0, 6.0, ((0, 4), (1, 8)), jnp.float32)
    return {"initial_realization_fields": initial_realization_fields, "measurement_location_offset": measurement_location_offset, "observed": observed, "obs_var": obs_var, "obs_noise": obs_noise}


alpha_mda = 4.0
buoyancy = 0.5
head_rate = 0.02
salt_diffusion = 0.01
salt_advection = 0.01

def neighbours(padded):
    return [padded[:, :-2, 1:-1, 1:-1], padded[:, 2:, 1:-1, 1:-1], padded[:, 1:-1, :-2, 1:-1], padded[:, 1:-1, 2:, 1:-1], padded[:, 1:-1, 1:-1, :-2], padded[:, 1:-1, 1:-1, 2:]]

def transport(cond_pad, head_pad, salt_pad):
    conduct = cond_pad[:, 1:-1, 1:-1, 1:-1]
    head_now = head_pad[:, 1:-1, 1:-1, 1:-1]
    salt_now = salt_pad[:, 1:-1, 1:-1, 1:-1]
    head_sum = jnp.zeros_like(head_now)
    salt_sum = jnp.zeros_like(salt_now)
    directions = (-1.0, 1.0, 0.0, 0.0, 0.0, 0.0)
    for buoyant, cond_nb, head_nb, salt_nb in zip(directions, neighbours(cond_pad), neighbours(head_pad), neighbours(salt_pad)):
        face_cond = 2.0 * conduct * cond_nb / (conduct + cond_nb)
        face_flux = face_cond * (head_nb - head_now + buoyant * buoyancy * 0.5 * (salt_now + salt_nb))
        head_sum = head_sum + face_flux
        salt_sum = salt_sum + salt_diffusion * face_cond * (salt_nb - salt_now) + salt_advection * face_flux * 0.5 * (salt_now + salt_nb)
    return (head_now + head_rate * head_sum, salt_now + salt_sum)

def reference(initial_realization_fields, measurement_location_offset, observed, obs_var, obs_noise):
    widths = ((0, 0), (1, 1), (1, 1), (1, 1))
    conduct = jnp.exp(initial_realization_fields[:, 0])
    stepped_hydraulic_level, stepped_solute_concentration = transport(jnp.pad(conduct, widths), jnp.pad(initial_realization_fields[:, 1], widths), jnp.pad(initial_realization_fields[:, 2], widths))
    trial_realization = jnp.stack([initial_realization_fields[:, 0], stepped_hydraulic_level, stepped_solute_concentration], axis=1)
    realization_stack = trial_realization.shape[0]
    modeled_readings = jnp.take(trial_realization[:, 1:3].reshape(realization_stack, -1), measurement_location_offset, axis=1)
    obs_scale = jnp.sqrt(alpha_mda * obs_var)
    innovation = (observed[None, :] - modeled_readings) / obs_scale[None, :] + obs_noise.T
    anomaly = (modeled_readings - lax.optimization_barrier(jnp.mean(modeled_readings, axis=0, keepdims=True))) / (obs_scale[None, :] * jnp.sqrt(jnp.float32(realization_stack - 1)))
    gram_sum = jnp.dot(anomaly.astype(jnp.float32), anomaly.T.astype(jnp.float32), precision=lax.Precision.HIGHEST, preferred_element_type=jnp.float32)
    cross_sum = jnp.dot(anomaly.astype(jnp.float32), innovation.T.astype(jnp.float32), precision=lax.Precision.HIGHEST, preferred_element_type=jnp.float32)
    identity = jnp.eye(realization_stack, dtype=jnp.float32)
    lower_factor = jnp.linalg.cholesky(identity + gram_sum)
    half_solve = lax.linalg.triangular_solve(lower_factor, cross_sum, left_side=True, lower=True)
    weights = lax.linalg.triangular_solve(lower_factor, half_solve, left_side=True, lower=True, transpose_a=True)
    scaled = weights / jnp.sqrt(jnp.float32(realization_stack - 1))
    blend_weight = identity + scaled - lax.optimization_barrier(jnp.mean(scaled, axis=0, keepdims=True))
    return jnp.tensordot(blend_weight.T, trial_realization, axes=1, precision=lax.Precision.HIGHEST)
```

```python
import functools
import math

import jax
import jax.numpy as jnp
from jax import lax
from jax.experimental import pallas as pl
from jax.experimental.pallas import tpu as pltpu
from jax.sharding import PartitionSpec as P

alpha_mda = 4.0
buoyancy = 0.5
head_rate = 0.02
salt_diffusion = 0.01
salt_advection = 0.01
HI = lax.Precision.HIGHEST
MESH = pl.DeviceIdType.MESH
VM = pl.BlockSpec(memory_space=pltpu.VMEM)


def forecast_kernel(x_ref, up_ref, dn_ref, row_ref, col_ref, fc_ref, pred_ref, k_ref):
    fields, layers, width, members, lanes = x_ref.shape
    groups = row_ref.shape[0]
    rank = lax.axis_index("tile")
    last = lax.axis_size("tile") - 1
    has_up = jnp.where(rank > 0, 1.0, 0.0).astype(jnp.float32)
    has_dn = jnp.where(rank < last, 1.0, 0.0).astype(jnp.float32)
    for l in range(layers):
        k_ref[l, 0] = jnp.exp(up_ref[0, l]) * has_up
        k_ref[l, width + 1] = jnp.exp(dn_ref[0, l]) * has_dn
        for r in range(width):
            k_ref[l, r + 1] = jnp.exp(x_ref[0, l, r])
    lane = lax.broadcasted_iota(jnp.int32, (members, lanes), 1)

    def cell(f, l, r):
        if r < 0:
            return up_ref[f, l]
        if r >= width:
            return dn_ref[f, l]
        return x_ref[f, l, r]

    def layer_row(l, r):
        k0, h0, c0 = k_ref[l, r + 1], x_ref[1, l, r], x_ref[2, l, r]
        hs = jnp.zeros_like(h0)
        cs = jnp.zeros_like(c0)
        near = []
        if l > 0:
            near.append((-1.0, k_ref[l - 1, r + 1], cell(1, l - 1, r), cell(2, l - 1, r)))
        if l < layers - 1:
            near.append((1.0, k_ref[l + 1, r + 1], cell(1, l + 1, r), cell(2, l + 1, r)))
        near.append((0.0, k_ref[l, r], cell(1, l, r - 1), cell(2, l, r - 1)))
        near.append((0.0, k_ref[l, r + 2], cell(1, l, r + 1), cell(2, l, r + 1)))
        near.append(
            (
                0.0,
                jnp.where(lane == 0, 0.0, pltpu.roll(k0, 1, 1)),
                pltpu.roll(h0, 1, 1),
                pltpu.roll(c0, 1, 1),
            )
        )
        near.append(
            (
                0.0,
                jnp.where(lane == lanes - 1, 0.0, pltpu.roll(k0, lanes - 1, 1)),
                pltpu.roll(h0, lanes - 1, 1),
                pltpu.roll(c0, lanes - 1, 1),
            )
        )
        for s, kn, hn, cn in near:
            g = 2.0 * k0 * kn / (k0 + kn)
            csum = c0 + cn
            drop = hn - h0
            if s != 0.0:
                drop = drop + (s * buoyancy * 0.5) * csum
            flux = g * drop
            hs = hs + flux
            cs = cs + salt_diffusion * g * (cn - c0) + salt_advection * flux * 0.5 * csum
        flat = l * width + r
        per = layers * width
        fc_ref[flat] = x_ref[0, l, r]
        fc_ref[per + flat] = h0 + head_rate * hs
        fc_ref[2 * per + flat] = c0 + cs

    for l in range(layers):
        for r in range(width):
            layer_row(l, r)
    rows = [jnp.broadcast_to(row_ref[g], (members, lanes)) for g in range(groups)]
    cols = [jnp.broadcast_to(col_ref[g], (members, lanes)) for g in range(groups)]
    per = layers * width
    step = 8
    for g0 in range(0, groups, step):
        part = range(g0, min(g0 + step, groups))

        def body(r, accs):
            v = fc_ref[per + r]
            return tuple(
                jnp.where(rows[g] == r, jnp.take_along_axis(v, cols[g], axis=1), a)
                for g, a in zip(part, accs)
            )

        accs = lax.fori_loop(
            0, 2 * per, body, tuple(jnp.zeros((members, lanes), jnp.float32) for _ in part)
        )
        for g, a in zip(part, accs):
            pred_ref[g] = a


def analysis_kernel(
    fc_ref, pred_ref, noise_ref, obs_ref, scale_ref, out_ref,
    pbuf, nbuf, part, rsbuf, gc, gbuf, obuf, sref, cref,
    s_pred, r_pred, s_noise, r_noise, s_fwd, r_fwd, s_rs, r_rs, s_ag, r_ag, s_back, r_back, s_loc,
):
    nm, nt = lax.axis_size("mem"), lax.axis_size("tile")
    n = nm * nt
    d, t = lax.axis_index("mem"), lax.axis_index("tile")
    me = d * nt + t
    gpc, members, lanes = pbuf.shape[2:]
    ncl = nm // nt
    total = nm * members
    reducers, blk, blk_lanes = gc.shape
    crows = gbuf.shape[0]
    worker = t == d // ncl

    def remote(src, dst, ss, rs, mem, tile):
        return pltpu.make_async_remote_copy(
            src_ref=src, dst_ref=dst, send_sem=ss, recv_sem=rs,
            device_id={"mem": mem, "tile": tile}, device_id_type=MESH,
        )

    def drain(ref, sem):
        pltpu.make_async_copy(ref, ref, sem).wait()

    barrier = pltpu.get_barrier_semaphore()

    def greet(i, _):
        to = lax.rem(me + i, n)
        pl.semaphore_signal(
            barrier, 1, device_id={"mem": to // nt, "tile": lax.rem(to, nt)}, device_id_type=MESH
        )
        return 0

    lax.fori_loop(1, n, greet, 0)
    pl.semaphore_wait(barrier, n - 1)

    for k in range(nm):
        c = lax.rem(d + k, nm)
        src = pred_ref.at[pl.ds(c * gpc, gpc)]
        if k == 0:
            @pl.when(worker)
            def _():
                pbuf[t, d] = pred_ref[pl.ds(d * gpc, gpc)]

            @pl.when(jnp.logical_not(worker))
            def _():
                remote(src, pbuf.at[t, d], s_pred, r_pred, c, c // ncl).start()
        else:
            remote(src, pbuf.at[t, d], s_pred, r_pred, c, c // ncl).start()
    for j in range(ncl):
        c = t * ncl + j
        src = noise_ref.at[pl.ds(j * gpc, gpc)]

        @pl.when(c != d)
        def _():
            remote(src, nbuf.at[d], s_noise, r_noise, c, t).start()

        @pl.when(c == d)
        def _():
            nbuf[d] = noise_ref[pl.ds(j * gpc, gpc)]

    mine = pl.ds(pl.multiple_of(d * members, members), members)
    for k in range(1, nm):
        c = lax.rem(d + k, nm)
        remote(
            fc_ref.at[pl.ds(c * crows, crows)], gbuf.at[:, mine, :], s_fwd, r_fwd, c, t
        ).start()
    local = pltpu.make_async_copy(
        fc_ref.at[pl.ds(d * crows, crows)], gbuf.at[:, mine, :], s_loc
    )
    local.start()

    @pl.when(worker)
    def _():
        drain(pbuf_flat(pbuf, n - 1), r_pred)
        drain(nbuf.at[pl.ds(0, nm - 1)], r_noise)
        gram = jnp.zeros((total, total), jnp.float32)
        cross = jnp.zeros((total, total), jnp.float32)
        base = lax.rem(d, ncl) * gpc
        for g in range(gpc):
            pred = pbuf[0, :, g]
            for q in range(1, nt):
                pred = pred + pbuf[q, :, g]
            pred = pred.reshape(total, lanes)
            noise = nbuf[:, g].reshape(total, lanes)
            scale = scale_ref[base + g]
            innov = (obs_ref[base + g] - pred) / scale + noise
            anom = (pred - jnp.mean(pred, axis=0, keepdims=True)) / (
                scale * math.sqrt(total - 1)
            )
            dims = (((1,), (1,)), ((), ()))
            gram = gram + lax.dot_general(
                anom, anom, dims, precision=HI, preferred_element_type=jnp.float32
            )
            cross = cross + lax.dot_general(
                anom, innov, dims, precision=HI, preferred_element_type=jnp.float32
            )
        half = reducers // 2
        part[pl.ds(0, half)] = gram.reshape(half, blk, blk_lanes)
        part[pl.ds(half, half)] = cross.reshape(half, blk, blk_lanes)

        def scatter(i, _):
            to = lax.rem(me + i, n)

            @pl.when(to < reducers)
            def _():
                remote(part.at[to], rsbuf.at[d], s_rs, r_rs, to // nt, lax.rem(to, nt)).start()
            return 0

        lax.fori_loop(1, n, scatter, 0)

        @pl.when(me < reducers)
        def _():
            rsbuf[d] = part[me]

    @pl.when(me < reducers)
    def _():
        @pl.when(worker)
        def _():
            drain(rsbuf.at[pl.ds(0, nm - 1)], r_rs)

        @pl.when(jnp.logical_not(worker))
        def _():
            drain(rsbuf, r_rs)
        acc = rsbuf[0]
        for q in range(1, nm):
            acc = acc + rsbuf[q]
        gc[me] = acc

        def spread(i, _):
            to = lax.rem(me + i, n)
            remote(gc.at[me], gc.at[me], s_ag, r_ag, to // nt, lax.rem(to, nt)).start()
            return 0

        lax.fori_loop(1, n, spread, 0)
        drain(gc.at[pl.ds(0, reducers - 1)], r_ag)

    if reducers < n:
        @pl.when(me >= reducers)
        def _():
            drain(gc, r_ag)

    half = reducers // 2
    eye = (
        lax.broadcasted_iota(jnp.int32, (total, total), 0)
        == lax.broadcasted_iota(jnp.int32, (total, total), 1)
    ).astype(jnp.float32)
    sref[...] = gc[pl.ds(0, half)].reshape(total, total) + eye
    cref[...] = gc[pl.ds(half, half)].reshape(total, total)
    b = 16
    blane = lax.broadcasted_iota(jnp.int32, (b, total), 1)
    brow = lax.broadcasted_iota(jnp.int32, (b, total), 0)
    flane = lax.broadcasted_iota(jnp.int32, (total, total), 1)

    def sweep(g, _):
        first = pl.multiple_of(g * b, b)
        rows = sref[pl.ds(first, b), :]
        z_c = cref[pl.ds(first, b), :]
        piv = pltpu.roll(rows, lax.rem(total - first, total), 1)
        own = (blane >= first) & (blane < first + b)
        z_s = jnp.where(own, jnp.where(blane == brow + first, -1.0, 0.0), rows)
        for k in range(b):
            inv = 1.0 / piv[k : k + 1, k : k + 1]
            col = piv[:, k : k + 1]
            fac = jnp.where(brow == k, 0.0, col)
            at = brow == k

            def upd(z):
                new = z[k : k + 1, :] * inv
                return jnp.where(at, new, z - fac * new)

            piv, z_s, z_c = upd(piv), upd(z_s), upd(z_c)
        left = rows.T
        keep = (flane >= first) & (flane < first + b)
        s_old = jnp.where(keep, 0.0, sref[...])
        s_new = s_old - jnp.dot(left, z_s, precision=HI, preferred_element_type=jnp.float32)
        c_new = cref[...] - jnp.dot(left, z_c, precision=HI, preferred_element_type=jnp.float32)
        sref[...] = s_new
        cref[...] = c_new
        sref[pl.ds(first, b), :] = z_s
        cref[pl.ds(first, b), :] = z_c
        return 0

    lax.fori_loop(0, total // b, sweep, 0)
    scaled = cref[...] / math.sqrt(total - 1)
    mix = (eye + scaled - jnp.mean(scaled, axis=0, keepdims=True)).T

    local.wait()
    drain(gbuf.at[:, pl.ds(0, (nm - 1) * members), :], r_fwd)
    parts = 3 if crows % 3 == 0 else 1
    pr = crows // parts
    for q in range(parts):
        for r in range(q * pr, (q + 1) * pr):
            obuf[r] = jnp.dot(mix, gbuf[r], precision=HI, preferred_element_type=jnp.float32)
        for k in range(1, nm):
            c = lax.rem(d + k, nm)
            theirs = pl.ds(pl.multiple_of(c * members, members), members)
            remote(
                obuf.at[pl.ds(q * pr, pr), theirs, :],
                out_ref.at[pl.ds(d * crows + q * pr, pr)],
                s_back, r_back, c, t,
            ).start()
    out_ref[pl.ds(d * crows, crows)] = obuf[:, mine, :]

    @pl.when(worker)
    def _():
        drain(pred_ref.at[pl.ds(0, (nm - 1) * gpc)], s_pred)
        if reducers < n:
            @pl.when(me < reducers)
            def _():
                drain(part.at[pl.ds(0, reducers - 1)], s_rs)

            @pl.when(me >= reducers)
            def _():
                drain(part, s_rs)
        else:
            drain(part.at[pl.ds(0, reducers - 1)], s_rs)

    @pl.when(jnp.logical_not(worker))
    def _():
        drain(pred_ref, s_pred)

    @pl.when(worker)
    def _():
        if ncl > 1:
            drain(noise_ref.at[pl.ds(0, (ncl - 1) * gpc)], s_noise)

    @pl.when(jnp.logical_not(worker))
    def _():
        drain(noise_ref, s_noise)

    @pl.when(me < reducers)
    def _():
        def done(i, _):
            drain(gc.at[0], s_ag)
            return 0

        if reducers == n:
            drain(gc.at[pl.ds(0, n - 1)], s_ag)
        else:
            lax.fori_loop(1, n, done, 0)
    drain(fc_ref.at[pl.ds(0, (nm - 1) * crows)], s_fwd)
    drain(obuf.at[:, pl.ds(0, (nm - 1) * members), :], s_back)
    drain(out_ref.at[pl.ds(0, (nm - 1) * crows)], r_back)


def pbuf_flat(ref, count):
    nt, nm = ref.shape[:2]
    return ref.reshape((nt * nm,) + ref.shape[2:]).at[pl.ds(0, count)]


def local(fields_in, offsets, observed, obs_var, obs_noise):
    members, fields, layers, width, lanes = fields_in.shape
    rank = lax.axis_index("tile")
    nt, nm = lax.axis_size("tile"), lax.axis_size("mem")
    n = nt * nm
    x = fields_in.transpose(1, 2, 3, 0, 4)
    up = lax.ppermute(x[:, :, width - 1], "tile", [(i, i + 1) for i in range(nt - 1)])
    dn = lax.ppermute(x[:, :, 0], "tile", [(i + 1, i) for i in range(nt - 1)])
    plane = width * nt * lanes
    lay = offsets // plane
    rest = offsets % plane
    lrow = rest // lanes - rank * width
    row = jnp.where((lrow >= 0) & (lrow < width), lay * width + lrow, -1)
    groups = offsets.shape[0] // lanes
    row = row.reshape(groups, 1, lanes)
    col = (rest % lanes).reshape(groups, 1, lanes)
    rows = fields * layers * width
    f32 = jnp.float32
    fc, pred = pl.pallas_call(
        forecast_kernel,
        out_shape=(
            jax.ShapeDtypeStruct((rows, members, lanes), f32),
            jax.ShapeDtypeStruct((groups, members, lanes), f32),
        ),
        in_specs=[VM] * 5,
        out_specs=(VM, VM),
        scratch_shapes=[pltpu.VMEM((layers, width + 2, members, lanes), f32)],
    )(x, up, dn, row, col)
    gpc = groups // nm
    own = groups // nt
    noise = obs_noise.reshape(own, lanes, members).transpose(0, 2, 1)
    obs = observed.reshape(own, 1, lanes)
    scale = jnp.sqrt(alpha_mda * obs_var).reshape(own, 1, lanes)
    total = members * nm
    reducers = min(n, 2 * total // 8)
    blk = 2 * total // reducers
    crows = rows // nm
    dma = pltpu.SemaphoreType.DMA
    out = pl.pallas_call(
        analysis_kernel,
        out_shape=jax.ShapeDtypeStruct((rows, members, lanes), f32),
        in_specs=[VM] * 5,
        out_specs=VM,
        scratch_shapes=[
            pltpu.VMEM((nt, nm, gpc, members, lanes), f32),
            pltpu.VMEM((nm, gpc, members, lanes), f32),
            pltpu.VMEM((reducers, blk, total), f32),
            pltpu.VMEM((nm, blk, total), f32),
            pltpu.VMEM((reducers, blk, total), f32),
            pltpu.VMEM((crows, total, lanes), f32),
            pltpu.VMEM((crows, total, lanes), f32),
            pltpu.VMEM((total, total), f32),
            pltpu.VMEM((total, total), f32),
        ]
        + [dma] * 13,
        compiler_params=pltpu.CompilerParams(collective_id=0, has_side_effects=True),
    )(fc, pred, noise, obs, scale)
    return out.reshape(fields, layers, width, members, lanes).transpose(3, 0, 1, 2, 4)


def solution(mesh):
    in_specs = (P("mem", None, None, "tile", None), P(), P("tile"), P("tile"), P("tile", "mem"))
    out_specs = P("mem", None, None, "tile", None)
    return jax.shard_map(local, mesh=mesh, in_specs=in_specs, out_specs=out_specs, check_vma=False)
```

```python
import functools
import math

import jax
import jax.numpy as jnp
from jax import lax
from jax.experimental import pallas as pl
from jax.experimental.pallas import tpu as pltpu
from jax.sharding import PartitionSpec as P

alpha_mda = 4.0
buoyancy = 0.5
head_rate = 0.02
salt_diffusion = 0.01
salt_advection = 0.01
HI = lax.Precision.HIGHEST
MESH = pl.DeviceIdType.MESH
VM = pl.BlockSpec(memory_space=pltpu.VMEM)


def face(a, b, buoyant):
    ka, ha, ca = a
    kb, hb, cb = b
    g = 2.0 * ka * kb / (ka + kb)
    csum = ca + cb
    drop = hb - ha
    if buoyant:
        drop = drop + (buoyancy * 0.5) * csum
    flux = g * drop
    return flux, salt_diffusion * g * (cb - ca) + (salt_advection * 0.5) * flux * csum


def step_inside(x_ref, fc_ref, k_ref, lay_ref):
    fields, layers, width, members, lanes = x_ref.shape
    per = layers * width
    lane = lax.broadcasted_iota(jnp.int32, (members, lanes), 1)
    for l in range(layers):
        for r in range(width):
            k_ref[l, r] = jnp.exp(x_ref[0, l, r])
    for l in range(layers):
        row_face = None
        for r in range(width):
            here = (k_ref[l, r], x_ref[1, l, r], x_ref[2, l, r])
            k0, h0, c0 = here
            right = (
                jnp.where(lane == lanes - 1, 0.0, pltpu.roll(k0, lanes - 1, 1)),
                pltpu.roll(h0, lanes - 1, 1),
                pltpu.roll(c0, lanes - 1, 1),
            )
            fh, fs = face(here, right, False)
            hs, cs = fh - pltpu.roll(fh, 1, 1), fs - pltpu.roll(fs, 1, 1)
            if row_face is not None:
                hs, cs = hs - row_face[0], cs - row_face[1]
            if r < width - 1:
                row_face = face(
                    here, (k_ref[l, r + 1], x_ref[1, l, r + 1], x_ref[2, l, r + 1]), False
                )
                hs, cs = hs + row_face[0], cs + row_face[1]
            if l > 0:
                hs, cs = hs - lay_ref[0, r], cs - lay_ref[1, r]
            if l < layers - 1:
                fh, fs = face(here, (k_ref[l + 1, r], x_ref[1, l + 1, r], x_ref[2, l + 1, r]), True)
                lay_ref[0, r] = fh
                lay_ref[1, r] = fs
                hs, cs = hs + fh, cs + fs
            flat = l * width + r
            fc_ref[flat] = x_ref[0, l, r]
            fc_ref[per + flat] = h0 + head_rate * hs
            fc_ref[2 * per + flat] = c0 + cs


def step_edges(x_ref, up_ref, dn_ref, fc_ref, k_ref, has_up, has_dn):
    fields, layers, width, members, lanes = x_ref.shape
    per = layers * width
    for l in range(layers):
        for r, halo, has, sign in ((0, up_ref, has_up, -1.0), (width - 1, dn_ref, has_dn, 1.0)):
            here = (k_ref[l, r], x_ref[1, l, r], x_ref[2, l, r])
            there = (jnp.exp(halo[0, l]) * has, halo[1, l], halo[2, l])
            fh, fs = face(here, there, False) if sign > 0 else face(there, here, False)
            flat = l * width + r
            fc_ref[per + flat] = fc_ref[per + flat] + (sign * head_rate) * fh
            fc_ref[2 * per + flat] = fc_ref[2 * per + flat] + sign * fs


def observe(fc_ref, row_ref, col_ref, pred_ref, per):
    groups = row_ref.shape[0]
    members, lanes = fc_ref.shape[1:]
    rows = [jnp.broadcast_to(row_ref[g], (members, lanes)) for g in range(groups)]
    cols = [jnp.broadcast_to(col_ref[g], (members, lanes)) for g in range(groups)]
    step = 8
    for g0 in range(0, groups, step):
        part = range(g0, min(g0 + step, groups))

        def body(r, accs):
            v = fc_ref[per + r]
            return tuple(
                jnp.where(rows[g] == r, jnp.take_along_axis(v, cols[g], axis=1), a)
                for g, a in zip(part, accs)
            )

        accs = lax.fori_loop(
            0, 2 * per, body, tuple(jnp.zeros((members, lanes), jnp.float32) for _ in part)
        )
        for g, a in zip(part, accs):
            pred_ref[g] = a


def analysis_kernel(
    x_ref, row_ref, col_ref, noise_ref, obs_ref, var_ref, out_ref,
    fc_ref, pred_ref, k_ref, lay_ref, up_ref, dn_ref, pbuf, nbuf, part, rsbuf, gc, gbuf, obuf, sref, cref,
    s_pred, r_pred, s_noise, r_noise, s_fwd, r_fwd, s_rs, r_rs, s_ag, r_ag, s_back, r_back, s_loc, s_up, r_up, s_dn, r_dn,
):
    nm, nt = lax.axis_size("mem"), lax.axis_size("tile")
    n = nm * nt
    d, t = lax.axis_index("mem"), lax.axis_index("tile")
    me = d * nt + t
    gpc, members, lanes = pbuf.shape[2:]
    ncl = nm // nt
    total = nm * members
    reducers, blk, blk_lanes = gc.shape
    crows = gbuf.shape[0]
    worker = t == d // ncl

    def remote(src, dst, ss, rs, mem, tile):
        return pltpu.make_async_remote_copy(
            src_ref=src, dst_ref=dst, send_sem=ss, recv_sem=rs,
            device_id={"mem": mem, "tile": tile}, device_id_type=MESH,
        )

    def drain(ref, sem):
        pltpu.make_async_copy(ref, ref, sem).wait()

    barrier = pltpu.get_barrier_semaphore()

    def greet(i, _):
        to = lax.rem(me + i, n)
        pl.semaphore_signal(
            barrier, 1, device_id={"mem": to // nt, "tile": lax.rem(to, nt)}, device_id_type=MESH
        )
        return 0

    lax.fori_loop(1, n, greet, 0)
    step_inside(x_ref, fc_ref, k_ref, lay_ref)
    pl.semaphore_wait(barrier, n - 1)

    fields, layers, width = x_ref.shape[:3]
    per = layers * width
    to_up = remote(x_ref.at[:, :, 0], dn_ref, s_up, r_up, d, jnp.maximum(t - 1, 0))
    to_dn = remote(x_ref.at[:, :, width - 1], up_ref, s_dn, r_dn, d, jnp.minimum(t + 1, nt - 1))

    @pl.when(t > 0)
    def _():
        to_up.start()

    @pl.when(t < nt - 1)
    def _():
        to_dn.start()

    @pl.when(t > 0)
    def _():
        to_dn.wait_recv()

    @pl.when(t == 0)
    def _():
        up_ref[...] = jnp.zeros_like(up_ref)

    @pl.when(t < nt - 1)
    def _():
        to_up.wait_recv()

    @pl.when(t == nt - 1)
    def _():
        dn_ref[...] = jnp.zeros_like(dn_ref)

    step_edges(
        x_ref, up_ref, dn_ref, fc_ref, k_ref,
        jnp.where(t > 0, 1.0, 0.0).astype(jnp.float32),
        jnp.where(t < nt - 1, 1.0, 0.0).astype(jnp.float32),
    )
    observe(fc_ref, row_ref, col_ref, pred_ref, per)

    for k in range(nm):
        c = lax.rem(d + k, nm)
        src = pred_ref.at[pl.ds(c * gpc, gpc)]
        if k == 0:
            @pl.when(worker)
            def _():
                pbuf[t, d] = pred_ref[pl.ds(d * gpc, gpc)]

            @pl.when(jnp.logical_not(worker))
            def _():
                remote(src, pbuf.at[t, d], s_pred, r_pred, c, c // ncl).start()
        else:
            remote(src, pbuf.at[t, d], s_pred, r_pred, c, c // ncl).start()
    for j in range(ncl):
        c = t * ncl + j
        src = noise_ref.at[pl.ds(j * gpc, gpc)]

        @pl.when(c != d)
        def _():
            remote(src, nbuf.at[d], s_noise, r_noise, c, t).start()

        @pl.when(c == d)
        def _():
            nbuf[d] = noise_ref[pl.ds(j * gpc, gpc)]

    mine = pl.ds(pl.multiple_of(d * members, members), members)

    def forward(first, count):
        for k in range(1, nm):
            c = lax.rem(d + k, nm)
            remote(
                fc_ref.at[pl.ds(c * crows + first, count)],
                gbuf.at[pl.ds(first, count), mine, :], s_fwd, r_fwd, c, t,
            ).start()

    early = crows // 3
    forward(0, early)
    local = pltpu.make_async_copy(
        fc_ref.at[pl.ds(d * crows, crows)], gbuf.at[:, mine, :], s_loc
    )
    local.start()

    @pl.when(worker)
    def _():
        drain(pbuf_flat(pbuf, n - 1), r_pred)
        drain(nbuf.at[pl.ds(0, nm - 1)], r_noise)
        gram = jnp.zeros((total, total), jnp.float32)
        cross = jnp.zeros((total, total), jnp.float32)
        base = lax.rem(d, ncl) * gpc
        for g in range(gpc):
            pred = pbuf[0, :, g]
            for q in range(1, nt):
                pred = pred + pbuf[q, :, g]
            pred = pred.reshape(total, lanes)
            noise = nbuf[:, g].reshape(total, lanes)
            scale = jnp.sqrt(alpha_mda * var_ref[base + g])
            innov = (obs_ref[base + g] - pred) / scale + noise
            anom = (pred - jnp.mean(pred, axis=0, keepdims=True)) / (
                scale * math.sqrt(total - 1)
            )
            dims = (((1,), (1,)), ((), ()))
            gram = gram + lax.dot_general(
                anom, anom, dims, precision=HI, preferred_element_type=jnp.float32
            )
            cross = cross + lax.dot_general(
                anom, innov, dims, precision=HI, preferred_element_type=jnp.float32
            )
        half = reducers // 2
        part[pl.ds(0, half)] = gram.reshape(half, blk, blk_lanes)
        part[pl.ds(half, half)] = cross.reshape(half, blk, blk_lanes)

        def scatter(i, _):
            to = lax.rem(me + i, n)

            @pl.when(to < reducers)
            def _():
                remote(part.at[to], rsbuf.at[d], s_rs, r_rs, to // nt, lax.rem(to, nt)).start()
            return 0

        lax.fori_loop(1, n, scatter, 0)

        @pl.when(me < reducers)
        def _():
            rsbuf[d] = part[me]

    @pl.when(me < reducers)
    def _():
        @pl.when(worker)
        def _():
            drain(rsbuf.at[pl.ds(0, nm - 1)], r_rs)

        @pl.when(jnp.logical_not(worker))
        def _():
            drain(rsbuf, r_rs)
        acc = rsbuf[0]
        for q in range(1, nm):
            acc = acc + rsbuf[q]
        gc[me] = acc

        def spread(i, _):
            to = lax.rem(me + i, n)
            remote(gc.at[me], gc.at[me], s_ag, r_ag, to // nt, lax.rem(to, nt)).start()
            return 0

        lax.fori_loop(1, n, spread, 0)

    forward(early, crows - early)

    @pl.when(me < reducers)
    def _():
        drain(gc.at[pl.ds(0, reducers - 1)], r_ag)

    if reducers < n:
        @pl.when(me >= reducers)
        def _():
            drain(gc, r_ag)

    half = reducers // 2
    eye = (
        lax.broadcasted_iota(jnp.int32, (total, total), 0)
        == lax.broadcasted_iota(jnp.int32, (total, total), 1)
    ).astype(jnp.float32)
    sref[...] = gc[pl.ds(0, half)].reshape(total, total) + eye
    cref[...] = gc[pl.ds(half, half)].reshape(total, total)
    b = 16
    blane = lax.broadcasted_iota(jnp.int32, (b, total), 1)
    brow = lax.broadcasted_iota(jnp.int32, (b, total), 0)
    flane = lax.broadcasted_iota(jnp.int32, (total, total), 1)

    def sweep(g, _):
        first = pl.multiple_of(g * b, b)
        rows = sref[pl.ds(first, b), :]
        z_c = cref[pl.ds(first, b), :]
        piv = pltpu.roll(rows, lax.rem(total - first, total), 1)
        own = (blane >= first) & (blane < first + b)
        z_s = jnp.where(own, jnp.where(blane == brow + first, -1.0, 0.0), rows)
        for k in range(0, b, 2):
            c0 = jnp.broadcast_to(piv[:, k : k + 1], (b, total))
            c1 = jnp.broadcast_to(piv[:, k + 1 : k + 2], (b, total))
            p00, p10 = c0[k : k + 1], c0[k + 1 : k + 2]
            p01, p11 = c1[k : k + 1], c1[k + 1 : k + 2]
            inv = 1.0 / (p00 * p11 - p01 * p10)
            pair = (brow == k) | (brow == k + 1)
            f0, f1 = jnp.where(pair, 0.0, c0), jnp.where(pair, 0.0, c1)

            def upd(z):
                z0, z1 = z[k : k + 1] * inv, z[k + 1 : k + 2] * inv
                n0 = p11 * z0 - p01 * z1
                n1 = p00 * z1 - p10 * z0
                rest = z - f0 * n0 - f1 * n1
                return jnp.where(brow == k, n0, jnp.where(brow == k + 1, n1, rest))

            piv, z_s, z_c = upd(piv), upd(z_s), upd(z_c)
        left = rows.T
        keep = (flane >= first) & (flane < first + b)
        s_old = jnp.where(keep, 0.0, sref[...])
        s_new = s_old - jnp.dot(left, z_s, precision=HI, preferred_element_type=jnp.float32)
        c_new = cref[...] - jnp.dot(left, z_c, precision=HI, preferred_element_type=jnp.float32)
        sref[...] = s_new
        cref[...] = c_new
        sref[pl.ds(first, b), :] = z_s
        cref[pl.ds(first, b), :] = z_c
        return 0

    lax.fori_loop(0, total // b, sweep, 0)
    scaled = cref[...] / math.sqrt(total - 1)
    mix = (eye + scaled - jnp.mean(scaled, axis=0, keepdims=True)).T

    local.wait()
    drain(gbuf.at[:, pl.ds(0, (nm - 1) * members), :], r_fwd)
    parts = 3 if crows % 3 == 0 else 1
    pr = crows // parts
    for q in range(parts):
        for r in range(q * pr, (q + 1) * pr):
            obuf[r] = jnp.dot(mix, gbuf[r], precision=HI, preferred_element_type=jnp.float32)
        for k in range(1, nm):
            c = lax.rem(d + k, nm)
            theirs = pl.ds(pl.multiple_of(c * members, members), members)
            remote(
                obuf.at[pl.ds(q * pr, pr), theirs, :],
                out_ref.at[pl.ds(d * crows + q * pr, pr)],
                s_back, r_back, c, t,
            ).start()
    out_ref[pl.ds(d * crows, crows)] = obuf[:, mine, :]

    @pl.when(t > 0)
    def _():
        to_up.wait_send()

    @pl.when(t < nt - 1)
    def _():
        to_dn.wait_send()

    @pl.when(worker)
    def _():
        drain(pred_ref.at[pl.ds(0, (nm - 1) * gpc)], s_pred)
        if reducers < n:
            @pl.when(me < reducers)
            def _():
                drain(part.at[pl.ds(0, reducers - 1)], s_rs)

            @pl.when(me >= reducers)
            def _():
                drain(part, s_rs)
        else:
            drain(part.at[pl.ds(0, reducers - 1)], s_rs)

    @pl.when(jnp.logical_not(worker))
    def _():
        drain(pred_ref, s_pred)

    @pl.when(worker)
    def _():
        if ncl > 1:
            drain(noise_ref.at[pl.ds(0, (ncl - 1) * gpc)], s_noise)

    @pl.when(jnp.logical_not(worker))
    def _():
        drain(noise_ref, s_noise)

    @pl.when(me < reducers)
    def _():
        def done(i, _):
            drain(gc.at[0], s_ag)
            return 0

        if reducers == n:
            drain(gc.at[pl.ds(0, n - 1)], s_ag)
        else:
            lax.fori_loop(1, n, done, 0)
    drain(fc_ref.at[pl.ds(0, (nm - 1) * crows)], s_fwd)
    drain(obuf.at[:, pl.ds(0, (nm - 1) * members), :], s_back)
    drain(out_ref.at[pl.ds(0, (nm - 1) * crows)], r_back)


def pbuf_flat(ref, count):
    nt, nm = ref.shape[:2]
    return ref.reshape((nt * nm,) + ref.shape[2:]).at[pl.ds(0, count)]


def local(fields_in, offsets, observed, obs_var, obs_noise):
    members, fields, layers, width, lanes = fields_in.shape
    rank = lax.axis_index("tile")
    nt, nm = lax.axis_size("tile"), lax.axis_size("mem")
    n = nt * nm
    x = fields_in.transpose(1, 2, 3, 0, 4)
    plane = width * nt * lanes
    lay = offsets // plane
    rest = offsets % plane
    lrow = rest // lanes - rank * width
    row = jnp.where((lrow >= 0) & (lrow < width), lay * width + lrow, -1)
    groups = offsets.shape[0] // lanes
    row = row.reshape(groups, 1, lanes)
    col = (rest % lanes).reshape(groups, 1, lanes)
    rows = fields * layers * width
    f32 = jnp.float32
    gpc = groups // nm
    own = groups // nt
    noise = obs_noise.reshape(own, lanes, members).transpose(0, 2, 1)
    obs = observed.reshape(own, 1, lanes)
    var = obs_var.reshape(own, 1, lanes)
    total = members * nm
    reducers = min(n, 2 * total // 8)
    blk = 2 * total // reducers
    crows = rows // nm
    dma = pltpu.SemaphoreType.DMA
    out = pl.pallas_call(
        analysis_kernel,
        out_shape=jax.ShapeDtypeStruct((rows, members, lanes), f32),
        in_specs=[VM] * 6,
        out_specs=VM,
        scratch_shapes=[
            pltpu.VMEM((rows, members, lanes), f32),
            pltpu.VMEM((groups, members, lanes), f32),
            pltpu.VMEM((layers, width, members, lanes), f32),
            pltpu.VMEM((2, width, members, lanes), f32),
            pltpu.VMEM((fields, layers, members, lanes), f32),
            pltpu.VMEM((fields, layers, members, lanes), f32),
            pltpu.VMEM((nt, nm, gpc, members, lanes), f32),
            pltpu.VMEM((nm, gpc, members, lanes), f32),
            pltpu.VMEM((reducers, blk, total), f32),
            pltpu.VMEM((nm, blk, total), f32),
            pltpu.VMEM((reducers, blk, total), f32),
            pltpu.VMEM((crows, total, lanes), f32),
            pltpu.VMEM((crows, total, lanes), f32),
            pltpu.VMEM((total, total), f32),
            pltpu.VMEM((total, total), f32),
        ]
        + [dma] * 17,
        compiler_params=pltpu.CompilerParams(collective_id=0, has_side_effects=True),
    )(x, row, col, noise, obs, var)
    return out.reshape(fields, layers, width, members, lanes).transpose(3, 0, 1, 2, 4)


def solution(mesh):
    in_specs = (P("mem", None, None, "tile", None), P(), P("tile"), P("tile"), P("tile", "mem"))
    out_specs = P("mem", None, None, "tile", None)
    return jax.shard_map(local, mesh=mesh, in_specs=in_specs, out_specs=out_specs, check_vma=False)
```

```python
import functools
import math

import jax
import jax.numpy as jnp
from jax import lax
from jax.experimental import pallas as pl
from jax.experimental.pallas import tpu as pltpu
from jax.sharding import PartitionSpec as P

alpha_mda = 4.0
buoyancy = 0.5
head_rate = 0.02
salt_diffusion = 0.01
salt_advection = 0.01
HI = lax.Precision.HIGHEST
MESH = pl.DeviceIdType.MESH
VM = pl.BlockSpec(memory_space=pltpu.VMEM)


def put(ref, flat, value):
    count = ref.shape[1]
    ref[flat // count, flat % count] = value


def get(ref, flat):
    count = ref.shape[1]
    return ref[flat // count, flat % count]


def face(a, b, buoyant):
    ka, ha, ca = a
    kb, hb, cb = b
    g = 2.0 * ka * kb / (ka + kb)
    csum = ca + cb
    drop = hb - ha
    if buoyant:
        drop = drop + (buoyancy * 0.5) * csum
    flux = g * drop
    return flux, salt_diffusion * g * (cb - ca) + (salt_advection * 0.5) * flux * csum


def step_inside(x_ref, fc_ref, k_ref, lay_ref):
    fields, layers, width, members, lanes = x_ref.shape
    per = layers * width
    lane = lax.broadcasted_iota(jnp.int32, (members, lanes), 1)
    for l in range(layers):
        for r in range(width):
            k_ref[l, r] = jnp.exp(x_ref[0, l, r])
    for l in range(layers):
        row_face = None
        for r in range(width):
            here = (k_ref[l, r], x_ref[1, l, r], x_ref[2, l, r])
            k0, h0, c0 = here
            right = (
                jnp.where(lane == lanes - 1, 0.0, pltpu.roll(k0, lanes - 1, 1)),
                pltpu.roll(h0, lanes - 1, 1),
                pltpu.roll(c0, lanes - 1, 1),
            )
            fh, fs = face(here, right, False)
            hs, cs = fh - pltpu.roll(fh, 1, 1), fs - pltpu.roll(fs, 1, 1)
            if row_face is not None:
                hs, cs = hs - row_face[0], cs - row_face[1]
            if r < width - 1:
                row_face = face(
                    here, (k_ref[l, r + 1], x_ref[1, l, r + 1], x_ref[2, l, r + 1]), False
                )
                hs, cs = hs + row_face[0], cs + row_face[1]
            if l > 0:
                hs, cs = hs - lay_ref[0, r], cs - lay_ref[1, r]
            if l < layers - 1:
                fh, fs = face(here, (k_ref[l + 1, r], x_ref[1, l + 1, r], x_ref[2, l + 1, r]), True)
                lay_ref[0, r] = fh
                lay_ref[1, r] = fs
                hs, cs = hs + fh, cs + fs
            flat = l * width + r
            put(fc_ref, per + flat, h0 + head_rate * hs)
            put(fc_ref, 2 * per + flat, c0 + cs)


def step_edges(x_ref, up_ref, dn_ref, fc_ref, k_ref, has_up, has_dn):
    fields, layers, width, members, lanes = x_ref.shape
    per = layers * width
    for l in range(layers):
        for r, halo, has, sign in ((0, up_ref, has_up, -1.0), (width - 1, dn_ref, has_dn, 1.0)):
            here = (k_ref[l, r], x_ref[1, l, r], x_ref[2, l, r])
            there = (jnp.exp(halo[0, l]) * has, halo[1, l], halo[2, l])
            fh, fs = face(here, there, False) if sign > 0 else face(there, here, False)
            flat = l * width + r
            put(fc_ref, per + flat, get(fc_ref, per + flat) + (sign * head_rate) * fh)
            put(fc_ref, 2 * per + flat, get(fc_ref, 2 * per + flat) + sign * fs)


def observe(fc_ref, row_ref, hot_ref, pred_ref, per):
    groups = row_ref.shape[0]
    nm, members, lanes = fc_ref.shape[1:]
    first = per // nm
    rows = [jnp.broadcast_to(row_ref[g], (members, lanes)) for g in range(groups)]
    for g0 in range(0, groups, 8):
        part = range(g0, min(g0 + 8, groups))
        hot = hot_ref[:, g0 * lanes : (part[-1] + 1) * lanes]
        acc = [jnp.zeros((members, lanes), jnp.float32) for _ in part]
        for j in range(2 * per // nm):
            v = fc_ref[first + j].reshape(nm * members, lanes)
            hi = v.astype(jnp.bfloat16)
            left = v - hi.astype(jnp.float32)
            mid = left.astype(jnp.bfloat16)
            low = (left - mid.astype(jnp.float32)).astype(jnp.bfloat16)
            picked = jnp.dot(
                jnp.concatenate([hi, mid, low], axis=1), hot, preferred_element_type=jnp.float32
            )
            for q in range(nm):
                block = picked[q * members : (q + 1) * members]
                for i, g in enumerate(part):
                    acc[i] = jnp.where(
                        rows[g] == j * nm + q, block[:, i * lanes : (i + 1) * lanes], acc[i]
                    )
        for i, g in enumerate(part):
            pred_ref[g] = acc[i]


def analysis_kernel(
    x_in, row_ref, col_ref, noise_in, obs_ref, var_ref, out_ref,
    x_ref, noise_ref, hot_ref, orow, fc_ref, pred_ref, k_ref, lay_ref, up_ref, dn_ref, pbuf, nbuf, part, rsbuf, gc, gbuf, obuf, sref, cref,
    s_pred, r_pred, s_noise, r_noise, s_fwd, r_fwd, s_rs, r_rs, s_ag, r_ag, s_back, r_back, s_loc, s_up, r_up, s_dn, r_dn,
):
    nm, nt = lax.axis_size("mem"), lax.axis_size("tile")
    n = nm * nt
    d, t = lax.axis_index("mem"), lax.axis_index("tile")
    me = d * nt + t
    gpc, members, lanes = pbuf.shape[2:]
    ncl = nm // nt
    total = nm * members
    reducers, blk, blk_lanes = gc.shape
    crows = gbuf.shape[0]
    worker = t == d // ncl

    def remote(src, dst, ss, rs, mem, tile):
        return pltpu.make_async_remote_copy(
            src_ref=src, dst_ref=dst, send_sem=ss, recv_sem=rs,
            device_id={"mem": mem, "tile": tile}, device_id_type=MESH,
        )

    def drain(ref, sem):
        pltpu.make_async_copy(ref, ref, sem).wait()

    barrier = pltpu.get_barrier_semaphore()

    def greet(i, _):
        to = lax.rem(me + i, n)
        pl.semaphore_signal(
            barrier, 1, device_id={"mem": to // nt, "tile": lax.rem(to, nt)}, device_id_type=MESH
        )
        return 0

    lax.fori_loop(1, n, greet, 0)
    fields, layers, width = x_ref.shape[:3]
    per = layers * width
    rows_all = fields * per
    for f in range(fields):
        for l in range(layers):
            for r in range(width):
                flat = f * per + l * width + r
                value = x_in[pl.ds(flat, members, stride=rows_all), :]
                x_ref[f, l, r] = value
                if f == 0:
                    put(fc_ref, flat, value)
    for g in range(noise_ref.shape[0]):
        noise_ref[g] = noise_in[pl.ds(g * lanes, lanes), :].T
    lane_of = lax.broadcasted_iota(jnp.int32, (lanes, lanes), 0)
    for g in range(col_ref.shape[0]):
        hot = jnp.where(lane_of == col_ref[g], 1.0, 0.0).astype(jnp.bfloat16)
        for piece in range(3):
            hot_ref[pl.ds(piece * lanes, lanes), pl.ds(g * lanes, lanes)] = hot
    step_inside(x_ref, fc_ref, k_ref, lay_ref)
    pl.semaphore_wait(barrier, n - 1)

    to_up = remote(x_ref.at[:, :, 0], dn_ref, s_up, r_up, d, jnp.maximum(t - 1, 0))
    to_dn = remote(x_ref.at[:, :, width - 1], up_ref, s_dn, r_dn, d, jnp.minimum(t + 1, nt - 1))

    @pl.when(t > 0)
    def _():
        to_up.start()

    @pl.when(t < nt - 1)
    def _():
        to_dn.start()

    mine = pl.ds(pl.multiple_of(d * members, members), members)

    def forward(first, end):
        for k in range(1, nm):
            c = lax.rem(d + k, nm)
            span = pl.ds(first, end - first)
            remote(fc_ref.at[span, c], gbuf.at[span, mine, :], s_fwd, r_fwd, c, t).start()

    stage_a = per // nm
    stage_b = stage_a + max(1, crows // 6)
    stage_c = stage_b + max(1, crows // 3)
    forward(0, stage_a)

    @pl.when(t > 0)
    def _():
        to_dn.wait_recv()

    @pl.when(t == 0)
    def _():
        up_ref[...] = jnp.zeros_like(up_ref)

    @pl.when(t < nt - 1)
    def _():
        to_up.wait_recv()

    @pl.when(t == nt - 1)
    def _():
        dn_ref[...] = jnp.zeros_like(dn_ref)

    step_edges(
        x_ref, up_ref, dn_ref, fc_ref, k_ref,
        jnp.where(t > 0, 1.0, 0.0).astype(jnp.float32),
        jnp.where(t < nt - 1, 1.0, 0.0).astype(jnp.float32),
    )
    forward(stage_a, stage_b)
    observe(fc_ref, row_ref, hot_ref, pred_ref, per)

    for k in range(nm):
        c = lax.rem(d + k, nm)
        src = pred_ref.at[pl.ds(c * gpc, gpc)]
        if k == 0:
            @pl.when(worker)
            def _():
                pbuf[t, d] = pred_ref[pl.ds(d * gpc, gpc)]

            @pl.when(jnp.logical_not(worker))
            def _():
                remote(src, pbuf.at[t, d], s_pred, r_pred, c, c // ncl).start()
        else:
            remote(src, pbuf.at[t, d], s_pred, r_pred, c, c // ncl).start()
    for j in range(ncl):
        c = t * ncl + j
        src = noise_ref.at[pl.ds(j * gpc, gpc)]

        @pl.when(c != d)
        def _():
            remote(src, nbuf.at[d], s_noise, r_noise, c, t).start()

        @pl.when(c == d)
        def _():
            nbuf[d] = noise_ref[pl.ds(j * gpc, gpc)]

    forward(stage_b, stage_c)

    @pl.when(worker)
    def _():
        drain(pbuf_flat(pbuf, n - 1), r_pred)
        drain(nbuf.at[pl.ds(0, nm - 1)], r_noise)
        gram = jnp.zeros((total, total), jnp.float32)
        cross = jnp.zeros((total, total), jnp.float32)
        base = lax.rem(d, ncl) * gpc
        for g in range(gpc):
            pred = pbuf[0, :, g]
            for q in range(1, nt):
                pred = pred + pbuf[q, :, g]
            pred = pred.reshape(total, lanes)
            noise = nbuf[:, g].reshape(total, lanes)
            scale = jnp.sqrt(alpha_mda * var_ref[base + g])
            innov = (obs_ref[base + g] - pred) / scale + noise
            anom = (pred - jnp.mean(pred, axis=0, keepdims=True)) / (
                scale * math.sqrt(total - 1)
            )
            dims = (((1,), (1,)), ((), ()))
            gram = gram + lax.dot_general(
                anom, anom, dims, precision=HI, preferred_element_type=jnp.float32
            )
            cross = cross + lax.dot_general(
                anom, innov, dims, precision=HI, preferred_element_type=jnp.float32
            )
        half = reducers // 2
        part[pl.ds(0, half)] = gram.reshape(half, blk, blk_lanes)
        part[pl.ds(half, half)] = cross.reshape(half, blk, blk_lanes)

        def scatter(i, _):
            to = lax.rem(me + i, n)

            @pl.when(to < reducers)
            def _():
                remote(part.at[to], rsbuf.at[d], s_rs, r_rs, to // nt, lax.rem(to, nt)).start()
            return 0

        lax.fori_loop(1, n, scatter, 0)

        @pl.when(me < reducers)
        def _():
            rsbuf[d] = part[me]

    @pl.when(me < reducers)
    def _():
        @pl.when(worker)
        def _():
            drain(rsbuf.at[pl.ds(0, nm - 1)], r_rs)

        @pl.when(jnp.logical_not(worker))
        def _():
            drain(rsbuf, r_rs)
        acc = rsbuf[0]
        for q in range(1, nm):
            acc = acc + rsbuf[q]
        gc[me] = acc

        def spread(i, _):
            to = lax.rem(me + i, n)
            remote(gc.at[me], gc.at[me], s_ag, r_ag, to // nt, lax.rem(to, nt)).start()
            return 0

        lax.fori_loop(1, n, spread, 0)

    forward(stage_c, crows)
    local = pltpu.make_async_copy(fc_ref.at[:, d], gbuf.at[:, mine, :], s_loc)
    local.start()

    @pl.when(me < reducers)
    def _():
        drain(gc.at[pl.ds(0, reducers - 1)], r_ag)

    if reducers < n:
        @pl.when(me >= reducers)
        def _():
            drain(gc, r_ag)

    half = reducers // 2
    eye = (
        lax.broadcasted_iota(jnp.int32, (total, total), 0)
        == lax.broadcasted_iota(jnp.int32, (total, total), 1)
    ).astype(jnp.float32)
    sref[...] = gc[pl.ds(0, half)].reshape(total, total) + eye
    cref[...] = gc[pl.ds(half, half)].reshape(total, total)
    b = 16
    blane = lax.broadcasted_iota(jnp.int32, (b, total), 1)
    brow = lax.broadcasted_iota(jnp.int32, (b, total), 0)
    flane = lax.broadcasted_iota(jnp.int32, (total, total), 1)

    def sweep(g, _):
        first = pl.multiple_of(g * b, b)
        rows = sref[pl.ds(first, b), :]
        z_c = cref[pl.ds(first, b), :]
        piv = pltpu.roll(rows, lax.rem(total - first, total), 1)
        own = (blane >= first) & (blane < first + b)
        z_s = jnp.where(own, jnp.where(blane == brow + first, -1.0, 0.0), rows)
        for k in range(0, b, 2):
            c0 = jnp.broadcast_to(piv[:, k : k + 1], (b, total))
            c1 = jnp.broadcast_to(piv[:, k + 1 : k + 2], (b, total))
            p00, p10 = c0[k : k + 1], c0[k + 1 : k + 2]
            p01, p11 = c1[k : k + 1], c1[k + 1 : k + 2]
            inv = 1.0 / (p00 * p11 - p01 * p10)
            pair = (brow == k) | (brow == k + 1)
            f0, f1 = jnp.where(pair, 0.0, c0), jnp.where(pair, 0.0, c1)

            def upd(z):
                z0, z1 = z[k : k + 1] * inv, z[k + 1 : k + 2] * inv
                n0 = p11 * z0 - p01 * z1
                n1 = p00 * z1 - p10 * z0
                rest = z - f0 * n0 - f1 * n1
                return jnp.where(brow == k, n0, jnp.where(brow == k + 1, n1, rest))

            piv, z_s, z_c = upd(piv), upd(z_s), upd(z_c)
        left = rows.T
        keep = (flane >= first) & (flane < first + b)
        s_old = jnp.where(keep, 0.0, sref[...])
        s_new = s_old - jnp.dot(left, z_s, precision=HI, preferred_element_type=jnp.float32)
        c_new = cref[...] - jnp.dot(left, z_c, precision=HI, preferred_element_type=jnp.float32)
        sref[...] = s_new
        cref[...] = c_new
        sref[pl.ds(first, b), :] = z_s
        cref[pl.ds(first, b), :] = z_c
        return 0

    lax.fori_loop(0, total // b, sweep, 0)
    scaled = cref[...] / math.sqrt(total - 1)
    mix = (eye + scaled - jnp.mean(scaled, axis=0, keepdims=True)).T

    local.wait()
    drain(gbuf.at[:, pl.ds(0, (nm - 1) * members), :], r_fwd)
    parts = 6 if crows % 6 == 0 else 1
    pr = crows // parts
    for q in range(parts):
        for r in range(q * pr, (q + 1) * pr):
            obuf[r] = jnp.dot(mix, gbuf[r], precision=HI, preferred_element_type=jnp.float32)
        for k in range(1, nm):
            c = lax.rem(d + k, nm)
            theirs = pl.ds(pl.multiple_of(c * members, members), members)
            remote(
                obuf.at[pl.ds(q * pr, pr), theirs, :],
                orow.at[pl.ds(q * pr, pr), d],
                s_back, r_back, c, t,
            ).start()
    orow[:, d] = obuf[:, mine, :]

    @pl.when(t > 0)
    def _():
        to_up.wait_send()

    @pl.when(t < nt - 1)
    def _():
        to_dn.wait_send()

    @pl.when(worker)
    def _():
        drain(pred_ref.at[pl.ds(0, (nm - 1) * gpc)], s_pred)
        if reducers < n:
            @pl.when(me < reducers)
            def _():
                drain(part.at[pl.ds(0, reducers - 1)], s_rs)

            @pl.when(me >= reducers)
            def _():
                drain(part, s_rs)
        else:
            drain(part.at[pl.ds(0, reducers - 1)], s_rs)

    @pl.when(jnp.logical_not(worker))
    def _():
        drain(pred_ref, s_pred)

    @pl.when(worker)
    def _():
        if ncl > 1:
            drain(noise_ref.at[pl.ds(0, (ncl - 1) * gpc)], s_noise)

    @pl.when(jnp.logical_not(worker))
    def _():
        drain(noise_ref, s_noise)

    @pl.when(me < reducers)
    def _():
        def done(i, _):
            drain(gc.at[0], s_ag)
            return 0

        if reducers == n:
            drain(gc.at[pl.ds(0, n - 1)], s_ag)
        else:
            lax.fori_loop(1, n, done, 0)
    drain(fc_ref.at[:, pl.ds(0, nm - 1)], s_fwd)
    drain(obuf.at[:, pl.ds(0, (nm - 1) * members), :], s_back)
    drain(orow.at[:, pl.ds(0, nm - 1)], r_back)
    for flat in range(rows_all):
        out_ref[pl.ds(flat, members, stride=rows_all), :] = get(orow, flat)


def pbuf_flat(ref, count):
    nt, nm = ref.shape[:2]
    return ref.reshape((nt * nm,) + ref.shape[2:]).at[pl.ds(0, count)]


def local(fields_in, offsets, observed, obs_var, obs_noise):
    members, fields, layers, width, lanes = fields_in.shape
    rank = lax.axis_index("tile")
    nt, nm = lax.axis_size("tile"), lax.axis_size("mem")
    n = nt * nm
    rows = fields * layers * width
    x = fields_in.reshape(members * rows, lanes)
    plane = width * nt * lanes
    lay = offsets // plane
    rest = offsets % plane
    lrow = rest // lanes - rank * width
    row = jnp.where((lrow >= 0) & (lrow < width), lay * width + lrow, -1)
    groups = offsets.shape[0] // lanes
    row = row.reshape(groups, 1, lanes)
    col = (rest % lanes).reshape(groups, 1, lanes)
    f32 = jnp.float32
    gpc = groups // nm
    own = groups // nt
    obs = observed.reshape(own, 1, lanes)
    var = obs_var.reshape(own, 1, lanes)
    total = members * nm
    reducers = min(n, 2 * total // 8)
    blk = 2 * total // reducers
    crows = rows // nm
    dma = pltpu.SemaphoreType.DMA
    out = pl.pallas_call(
        analysis_kernel,
        out_shape=jax.ShapeDtypeStruct((members * rows, lanes), f32),
        in_specs=[VM] * 6,
        out_specs=VM,
        scratch_shapes=[
            pltpu.VMEM((fields, layers, width, members, lanes), f32),
            pltpu.VMEM((own, members, lanes), f32),
            pltpu.VMEM((3 * lanes, groups * lanes), jnp.bfloat16),
            pltpu.VMEM((crows, nm, members, lanes), f32),
            pltpu.VMEM((crows, nm, members, lanes), f32),
            pltpu.VMEM((groups, members, lanes), f32),
            pltpu.VMEM((layers, width, members, lanes), f32),
            pltpu.VMEM((2, width, members, lanes), f32),
            pltpu.VMEM((fields, layers, members, lanes), f32),
            pltpu.VMEM((fields, layers, members, lanes), f32),
            pltpu.VMEM((nt, nm, gpc, members, lanes), f32),
            pltpu.VMEM((nm, gpc, members, lanes), f32),
            pltpu.VMEM((reducers, blk, total), f32),
            pltpu.VMEM((nm, blk, total), f32),
            pltpu.VMEM((reducers, blk, total), f32),
            pltpu.VMEM((crows, total, lanes), f32),
            pltpu.VMEM((crows, total, lanes), f32),
            pltpu.VMEM((total, total), f32),
            pltpu.VMEM((total, total), f32),
        ]
        + [dma] * 17,
        compiler_params=pltpu.CompilerParams(collective_id=0, has_side_effects=True),
    )(x, row, col, obs_noise, obs, var)
    return out.reshape(fields_in.shape)


def solution(mesh):
    in_specs = (P("mem", None, None, "tile", None), P(), P("tile"), P("tile"), P("tile", "mem"))
    out_specs = P("mem", None, None, "tile", None)
    return jax.shard_map(local, mesh=mesh, in_specs=in_specs, out_specs=out_specs, check_vma=False)
```

```python
import functools
import math

import jax
import jax.numpy as jnp
from jax import lax
from jax.experimental import pallas as pl
from jax.experimental.pallas import tpu as pltpu
from jax.sharding import PartitionSpec as P

alpha_mda = 4.0
buoyancy = 0.5
head_rate = 0.02
salt_diffusion = 0.01
salt_advection = 0.01
HI = lax.Precision.HIGHEST
MESH = pl.DeviceIdType.MESH
VM = pl.BlockSpec(memory_space=pltpu.VMEM)


def put(ref, flat, value):
    count = ref.shape[1]
    ref[flat // count, flat % count] = value


def get(ref, flat):
    count = ref.shape[1]
    return ref[flat // count, flat % count]


def face(a, b, buoyant):
    ka, ha, ca = a
    kb, hb, cb = b
    g = 2.0 * ka * kb / (ka + kb)
    csum = ca + cb
    drop = hb - ha
    if buoyant:
        drop = drop + (buoyancy * 0.5) * csum
    flux = g * drop
    return flux, salt_diffusion * g * (cb - ca) + (salt_advection * 0.5) * flux * csum


def step_inside(x_ref, fc_ref, k_ref, lay_ref):
    fields, layers, width, members, lanes = x_ref.shape
    per = layers * width
    lane = lax.broadcasted_iota(jnp.int32, (members, lanes), 1)
    for l in range(layers):
        for r in range(width):
            k_ref[l, r] = jnp.exp(x_ref[0, l, r])
    for l in range(layers):
        row_face = None
        for r in range(width):
            here = (k_ref[l, r], x_ref[1, l, r], x_ref[2, l, r])
            k0, h0, c0 = here
            right = (
                jnp.where(lane == lanes - 1, 0.0, pltpu.roll(k0, lanes - 1, 1)),
                pltpu.roll(h0, lanes - 1, 1),
                pltpu.roll(c0, lanes - 1, 1),
            )
            fh, fs = face(here, right, False)
            hs, cs = fh - pltpu.roll(fh, 1, 1), fs - pltpu.roll(fs, 1, 1)
            if row_face is not None:
                hs, cs = hs - row_face[0], cs - row_face[1]
            if r < width - 1:
                row_face = face(
                    here, (k_ref[l, r + 1], x_ref[1, l, r + 1], x_ref[2, l, r + 1]), False
                )
                hs, cs = hs + row_face[0], cs + row_face[1]
            if l > 0:
                hs, cs = hs - lay_ref[0, r], cs - lay_ref[1, r]
            if l < layers - 1:
                fh, fs = face(here, (k_ref[l + 1, r], x_ref[1, l + 1, r], x_ref[2, l + 1, r]), True)
                lay_ref[0, r] = fh
                lay_ref[1, r] = fs
                hs, cs = hs + fh, cs + fs
            flat = l * width + r
            put(fc_ref, per + flat, h0 + head_rate * hs)
            put(fc_ref, 2 * per + flat, c0 + cs)


def step_edges(x_ref, up_ref, dn_ref, fc_ref, k_ref, has_up, has_dn):
    fields, layers, width, members, lanes = x_ref.shape
    per = layers * width
    for l in range(layers):
        for r, halo, has, sign in ((0, up_ref, has_up, -1.0), (width - 1, dn_ref, has_dn, 1.0)):
            here = (k_ref[l, r], x_ref[1, l, r], x_ref[2, l, r])
            there = (jnp.exp(halo[0, l]) * has, halo[1, l], halo[2, l])
            fh, fs = face(here, there, False) if sign > 0 else face(there, here, False)
            flat = l * width + r
            put(fc_ref, per + flat, get(fc_ref, per + flat) + (sign * head_rate) * fh)
            put(fc_ref, 2 * per + flat, get(fc_ref, 2 * per + flat) + sign * fs)


def observe(fc_ref, row_ref, hot_ref, pred_ref, per):
    groups = row_ref.shape[0]
    nm, members, lanes = fc_ref.shape[1:]
    first = per // nm
    rows = [jnp.broadcast_to(row_ref[g], (members, lanes)) for g in range(groups)]
    for g0 in range(0, groups, 8):
        part = range(g0, min(g0 + 8, groups))
        hot = hot_ref[:, g0 * lanes : (part[-1] + 1) * lanes]
        acc = [jnp.zeros((members, lanes), jnp.float32) for _ in part]
        for j in range(2 * per // nm):
            v = fc_ref[first + j].reshape(nm * members, lanes)
            hi = v.astype(jnp.bfloat16)
            left = v - hi.astype(jnp.float32)
            mid = left.astype(jnp.bfloat16)
            low = (left - mid.astype(jnp.float32)).astype(jnp.bfloat16)
            picked = jnp.dot(
                jnp.concatenate([hi, mid, low], axis=1), hot, preferred_element_type=jnp.float32
            )
            for q in range(nm):
                block = picked[q * members : (q + 1) * members]
                for i, g in enumerate(part):
                    acc[i] = jnp.where(
                        rows[g] == j * nm + q, block[:, i * lanes : (i + 1) * lanes], acc[i]
                    )
        for i, g in enumerate(part):
            pred_ref[g] = acc[i]


def analysis_kernel(
    x_in, row_ref, col_ref, noise_in, obs_ref, var_ref, out_ref,
    x_ref, noise_ref, hot_ref, orow, fc_ref, pred_ref, k_ref, lay_ref, up_ref, dn_ref, pbuf, nbuf, part, rsbuf, gc, gbuf, obuf, sref, cref,
    s_pred, r_pred, s_noise, r_noise, s_fwd, r_fwd, s_rs, r_rs, s_ag, r_ag, s_back, r_back, s_loc, s_up, r_up, s_dn, r_dn,
):
    nm, nt = lax.axis_size("mem"), lax.axis_size("tile")
    n = nm * nt
    d, t = lax.axis_index("mem"), lax.axis_index("tile")
    me = d * nt + t
    gpc, members, lanes = pbuf.shape[2:]
    ncl = nm // nt
    total = nm * members
    reducers, blk, blk_lanes = gc.shape
    crows = gbuf.shape[0]
    worker = t == d // ncl

    def remote(src, dst, ss, rs, mem, tile):
        return pltpu.make_async_remote_copy(
            src_ref=src, dst_ref=dst, send_sem=ss, recv_sem=rs,
            device_id={"mem": mem, "tile": tile}, device_id_type=MESH,
        )

    def drain(ref, sem):
        pltpu.make_async_copy(ref, ref, sem).wait()

    barrier = pltpu.get_barrier_semaphore()

    def greet(i, _):
        to = lax.rem(me + i, n)
        pl.semaphore_signal(
            barrier, 1, device_id={"mem": to // nt, "tile": lax.rem(to, nt)}, device_id_type=MESH
        )
        return 0

    lax.fori_loop(1, n, greet, 0)
    fields, layers, width = x_ref.shape[:3]
    per = layers * width
    rows_all = fields * per
    for f in range(fields):
        for l in range(layers):
            for r in range(width):
                flat = f * per + l * width + r
                value = x_in[pl.ds(flat, members, stride=rows_all), :]
                x_ref[f, l, r] = value
                if f == 0:
                    put(fc_ref, flat, value)
    for g in range(noise_ref.shape[0]):
        noise_ref[g] = noise_in[pl.ds(g * lanes, lanes), :].T
    lane_of = lax.broadcasted_iota(jnp.int32, (lanes, lanes), 0)
    for g in range(col_ref.shape[0]):
        hot = jnp.where(lane_of == col_ref[g], 1.0, 0.0).astype(jnp.bfloat16)
        for piece in range(3):
            hot_ref[pl.ds(piece * lanes, lanes), pl.ds(g * lanes, lanes)] = hot
    step_inside(x_ref, fc_ref, k_ref, lay_ref)
    pl.semaphore_wait(barrier, n - 1)

    to_up = remote(x_ref.at[:, :, 0], dn_ref, s_up, r_up, d, jnp.maximum(t - 1, 0))
    to_dn = remote(x_ref.at[:, :, width - 1], up_ref, s_dn, r_dn, d, jnp.minimum(t + 1, nt - 1))

    @pl.when(t > 0)
    def _():
        to_up.start()

    @pl.when(t < nt - 1)
    def _():
        to_dn.start()

    mine = pl.ds(pl.multiple_of(d * members, members), members)

    def forward(first, end):
        for k in range(1, nm):
            c = lax.rem(d + k, nm)
            span = pl.ds(first, end - first)
            remote(fc_ref.at[span, c], gbuf.at[span, mine, :], s_fwd, r_fwd, c, t).start()

    @pl.when(t > 0)
    def _():
        to_dn.wait_recv()

    @pl.when(t == 0)
    def _():
        up_ref[...] = jnp.zeros_like(up_ref)

    @pl.when(t < nt - 1)
    def _():
        to_up.wait_recv()

    @pl.when(t == nt - 1)
    def _():
        dn_ref[...] = jnp.zeros_like(dn_ref)

    step_edges(
        x_ref, up_ref, dn_ref, fc_ref, k_ref,
        jnp.where(t > 0, 1.0, 0.0).astype(jnp.float32),
        jnp.where(t < nt - 1, 1.0, 0.0).astype(jnp.float32),
    )
    observe(fc_ref, row_ref, hot_ref, pred_ref, per)

    for k in range(nm):
        c = lax.rem(d + k, nm)
        src = pred_ref.at[pl.ds(c * gpc, gpc)]
        if k == 0:
            @pl.when(worker)
            def _():
                pbuf[t, d] = pred_ref[pl.ds(d * gpc, gpc)]

            @pl.when(jnp.logical_not(worker))
            def _():
                remote(src, pbuf.at[t, d], s_pred, r_pred, c, c // ncl).start()
        else:
            remote(src, pbuf.at[t, d], s_pred, r_pred, c, c // ncl).start()
    for j in range(ncl):
        c = t * ncl + j
        src = noise_ref.at[pl.ds(j * gpc, gpc)]

        @pl.when(c != d)
        def _():
            remote(src, nbuf.at[d], s_noise, r_noise, c, t).start()

        @pl.when(c == d)
        def _():
            nbuf[d] = noise_ref[pl.ds(j * gpc, gpc)]

    early = max(1, crows // 4)
    forward(0, early)

    @pl.when(worker)
    def _():
        drain(pbuf_flat(pbuf, n - 1), r_pred)
        drain(nbuf.at[pl.ds(0, nm - 1)], r_noise)
        gram = jnp.zeros((total, total), jnp.float32)
        cross = jnp.zeros((total, total), jnp.float32)
        base = lax.rem(d, ncl) * gpc
        for g in range(gpc):
            pred = pbuf[0, :, g]
            for q in range(1, nt):
                pred = pred + pbuf[q, :, g]
            pred = pred.reshape(total, lanes)
            noise = nbuf[:, g].reshape(total, lanes)
            scale = jnp.sqrt(alpha_mda * var_ref[base + g])
            innov = (obs_ref[base + g] - pred) / scale + noise
            anom = (pred - jnp.mean(pred, axis=0, keepdims=True)) / (
                scale * math.sqrt(total - 1)
            )
            dims = (((1,), (1,)), ((), ()))
            gram = gram + lax.dot_general(
                anom, anom, dims, precision=HI, preferred_element_type=jnp.float32
            )
            cross = cross + lax.dot_general(
                anom, innov, dims, precision=HI, preferred_element_type=jnp.float32
            )
        half = reducers // 2
        part[pl.ds(0, half)] = gram.reshape(half, blk, blk_lanes)
        part[pl.ds(half, half)] = cross.reshape(half, blk, blk_lanes)

        def scatter(i, _):
            to = lax.rem(me + i, n)

            @pl.when(to < reducers)
            def _():
                remote(part.at[to], rsbuf.at[d], s_rs, r_rs, to // nt, lax.rem(to, nt)).start()
            return 0

        lax.fori_loop(1, n, scatter, 0)

        @pl.when(me < reducers)
        def _():
            rsbuf[d] = part[me]

    @pl.when(me < reducers)
    def _():
        @pl.when(worker)
        def _():
            drain(rsbuf.at[pl.ds(0, nm - 1)], r_rs)

        @pl.when(jnp.logical_not(worker))
        def _():
            drain(rsbuf, r_rs)
        acc = rsbuf[0]
        for q in range(1, nm):
            acc = acc + rsbuf[q]
        gc[me] = acc

        def spread(i, _):
            to = lax.rem(me + i, n)
            remote(gc.at[me], gc.at[me], s_ag, r_ag, to // nt, lax.rem(to, nt)).start()
            return 0

        lax.fori_loop(1, n, spread, 0)

    forward(early, crows)
    local = pltpu.make_async_copy(fc_ref.at[:, d], gbuf.at[:, mine, :], s_loc)
    local.start()

    @pl.when(me < reducers)
    def _():
        drain(gc.at[pl.ds(0, reducers - 1)], r_ag)

    if reducers < n:
        @pl.when(me >= reducers)
        def _():
            drain(gc, r_ag)

    half = reducers // 2
    eye = (
        lax.broadcasted_iota(jnp.int32, (total, total), 0)
        == lax.broadcasted_iota(jnp.int32, (total, total), 1)
    ).astype(jnp.float32)
    sref[...] = gc[pl.ds(0, half)].reshape(total, total) + eye
    cref[...] = gc[pl.ds(half, half)].reshape(total, total)
    b = 16
    blane = lax.broadcasted_iota(jnp.int32, (b, total), 1)
    brow = lax.broadcasted_iota(jnp.int32, (b, total), 0)
    flane = lax.broadcasted_iota(jnp.int32, (total, total), 1)

    def sweep(g, _):
        first = pl.multiple_of(g * b, b)
        rows = sref[pl.ds(first, b), :]
        z_c = cref[pl.ds(first, b), :]
        piv = pltpu.roll(rows, lax.rem(total - first, total), 1)
        own = (blane >= first) & (blane < first + b)
        z_s = jnp.where(own, jnp.where(blane == brow + first, -1.0, 0.0), rows)
        for k in range(0, b, 2):
            c0 = jnp.broadcast_to(piv[:, k : k + 1], (b, total))
            c1 = jnp.broadcast_to(piv[:, k + 1 : k + 2], (b, total))
            p00, p10 = c0[k : k + 1], c0[k + 1 : k + 2]
            p01, p11 = c1[k : k + 1], c1[k + 1 : k + 2]
            inv = 1.0 / (p00 * p11 - p01 * p10)
            pair = (brow == k) | (brow == k + 1)
            f0, f1 = jnp.where(pair, 0.0, c0), jnp.where(pair, 0.0, c1)

            def upd(z):
                z0, z1 = z[k : k + 1] * inv, z[k + 1 : k + 2] * inv
                n0 = p11 * z0 - p01 * z1
                n1 = p00 * z1 - p10 * z0
                rest = z - f0 * n0 - f1 * n1
                return jnp.where(brow == k, n0, jnp.where(brow == k + 1, n1, rest))

            piv, z_s, z_c = upd(piv), upd(z_s), upd(z_c)
        left = rows.T
        keep = (flane >= first) & (flane < first + b)
        s_old = jnp.where(keep, 0.0, sref[...])
        s_new = s_old - jnp.dot(left, z_s, precision=HI, preferred_element_type=jnp.float32)
        c_new = cref[...] - jnp.dot(left, z_c, precision=HI, preferred_element_type=jnp.float32)
        sref[...] = s_new
        cref[...] = c_new
        sref[pl.ds(first, b), :] = z_s
        cref[pl.ds(first, b), :] = z_c
        return 0

    lax.fori_loop(0, total // b, sweep, 0)
    scaled = cref[...] / math.sqrt(total - 1)
    mix = (eye + scaled - jnp.mean(scaled, axis=0, keepdims=True)).T

    local.wait()
    drain(gbuf.at[:, pl.ds(0, (nm - 1) * members), :], r_fwd)
    parts = 3 if crows % 3 == 0 else 1
    pr = crows // parts
    for q in range(parts):
        for r in range(q * pr, (q + 1) * pr):
            obuf[r] = jnp.dot(mix, gbuf[r], precision=HI, preferred_element_type=jnp.float32)
        for k in range(1, nm):
            c = lax.rem(d + k, nm)
            theirs = pl.ds(pl.multiple_of(c * members, members), members)
            remote(
                obuf.at[pl.ds(q * pr, pr), theirs, :],
                orow.at[pl.ds(q * pr, pr), d],
                s_back, r_back, c, t,
            ).start()
    orow[:, d] = obuf[:, mine, :]

    @pl.when(t > 0)
    def _():
        to_up.wait_send()

    @pl.when(t < nt - 1)
    def _():
        to_dn.wait_send()

    @pl.when(worker)
    def _():
        drain(pred_ref.at[pl.ds(0, (nm - 1) * gpc)], s_pred)
        if reducers < n:
            @pl.when(me < reducers)
            def _():
                drain(part.at[pl.ds(0, reducers - 1)], s_rs)

            @pl.when(me >= reducers)
            def _():
                drain(part, s_rs)
        else:
            drain(part.at[pl.ds(0, reducers - 1)], s_rs)

    @pl.when(jnp.logical_not(worker))
    def _():
        drain(pred_ref, s_pred)

    @pl.when(worker)
    def _():
        if ncl > 1:
            drain(noise_ref.at[pl.ds(0, (ncl - 1) * gpc)], s_noise)

    @pl.when(jnp.logical_not(worker))
    def _():
        drain(noise_ref, s_noise)

    @pl.when(me < reducers)
    def _():
        def done(i, _):
            drain(gc.at[0], s_ag)
            return 0

        if reducers == n:
            drain(gc.at[pl.ds(0, n - 1)], s_ag)
        else:
            lax.fori_loop(1, n, done, 0)
    drain(fc_ref.at[:, pl.ds(0, nm - 1)], s_fwd)
    drain(obuf.at[:, pl.ds(0, (nm - 1) * members), :], s_back)
    drain(orow.at[:, pl.ds(0, nm - 1)], r_back)
    for flat in range(rows_all):
        out_ref[pl.ds(flat, members, stride=rows_all), :] = get(orow, flat)


def pbuf_flat(ref, count):
    nt, nm = ref.shape[:2]
    return ref.reshape((nt * nm,) + ref.shape[2:]).at[pl.ds(0, count)]


def local(fields_in, offsets, observed, obs_var, obs_noise):
    members, fields, layers, width, lanes = fields_in.shape
    rank = lax.axis_index("tile")
    nt, nm = lax.axis_size("tile"), lax.axis_size("mem")
    n = nt * nm
    rows = fields * layers * width
    x = fields_in.reshape(members * rows, lanes)
    plane = width * nt * lanes
    lay = offsets // plane
    rest = offsets % plane
    lrow = rest // lanes - rank * width
    row = jnp.where((lrow >= 0) & (lrow < width), lay * width + lrow, -1)
    groups = offsets.shape[0] // lanes
    row = row.reshape(groups, 1, lanes)
    col = (rest % lanes).reshape(groups, 1, lanes)
    f32 = jnp.float32
    gpc = groups // nm
    own = groups // nt
    obs = observed.reshape(own, 1, lanes)
    var = obs_var.reshape(own, 1, lanes)
    total = members * nm
    reducers = min(n, 2 * total // 8)
    blk = 2 * total // reducers
    crows = rows // nm
    dma = pltpu.SemaphoreType.DMA
    out = pl.pallas_call(
        analysis_kernel,
        out_shape=jax.ShapeDtypeStruct((members * rows, lanes), f32),
        in_specs=[VM] * 6,
        out_specs=VM,
        scratch_shapes=[
            pltpu.VMEM((fields, layers, width, members, lanes), f32),
            pltpu.VMEM((own, members, lanes), f32),
            pltpu.VMEM((3 * lanes, groups * lanes), jnp.bfloat16),
            pltpu.VMEM((crows, nm, members, lanes), f32),
            pltpu.VMEM((crows, nm, members, lanes), f32),
            pltpu.VMEM((groups, members, lanes), f32),
            pltpu.VMEM((layers, width, members, lanes), f32),
            pltpu.VMEM((2, width, members, lanes), f32),
            pltpu.VMEM((fields, layers, members, lanes), f32),
            pltpu.VMEM((fields, layers, members, lanes), f32),
            pltpu.VMEM((nt, nm, gpc, members, lanes), f32),
            pltpu.VMEM((nm, gpc, members, lanes), f32),
            pltpu.VMEM((reducers, blk, total), f32),
            pltpu.VMEM((nm, blk, total), f32),
            pltpu.VMEM((reducers, blk, total), f32),
            pltpu.VMEM((crows, total, lanes), f32),
            pltpu.VMEM((crows, total, lanes), f32),
            pltpu.VMEM((total, total), f32),
            pltpu.VMEM((total, total), f32),
        ]
        + [dma] * 17,
        compiler_params=pltpu.CompilerParams(collective_id=0, has_side_effects=True),
    )(x, row, col, obs_noise, obs, var)
    return out.reshape(fields_in.shape)


def solution(mesh):
    in_specs = (P("mem", None, None, "tile", None), P(), P("tile"), P("tile"), P("tile", "mem"))
    out_specs = P("mem", None, None, "tile", None)
    return jax.shard_map(local, mesh=mesh, in_specs=in_specs, out_specs=out_specs, check_vma=False)
```

```python
import functools
import math

import jax
import jax.numpy as jnp
from jax import lax
from jax.experimental import pallas as pl
from jax.experimental.pallas import tpu as pltpu
from jax.sharding import PartitionSpec as P

alpha_mda = 4.0
buoyancy = 0.5
head_rate = 0.02
salt_diffusion = 0.01
salt_advection = 0.01
HI = lax.Precision.HIGHEST
MESH = pl.DeviceIdType.MESH
VM = pl.BlockSpec(memory_space=pltpu.VMEM)


def put(ref, flat, value):
    count = ref.shape[1]
    ref[flat // count, flat % count] = value


def get(ref, flat):
    count = ref.shape[1]
    return ref[flat // count, flat % count]


def face(a, b, buoyant):
    ka, ha, ca = a
    kb, hb, cb = b
    g = 2.0 * ka * kb / (ka + kb)
    csum = ca + cb
    drop = hb - ha
    if buoyant:
        drop = drop + (buoyancy * 0.5) * csum
    flux = g * drop
    return flux, salt_diffusion * g * (cb - ca) + (salt_advection * 0.5) * flux * csum


def step_inside(x_ref, fc_ref, k_ref, lay_ref):
    fields, layers, width, members, lanes = x_ref.shape
    per = layers * width
    lane = lax.broadcasted_iota(jnp.int32, (members, lanes), 1)
    for l in range(layers):
        for r in range(width):
            k_ref[l, r] = jnp.exp(x_ref[0, l, r])
    for l in range(layers):
        row_face = None
        for r in range(width):
            here = (k_ref[l, r], x_ref[1, l, r], x_ref[2, l, r])
            k0, h0, c0 = here
            right = (
                jnp.where(lane == lanes - 1, 0.0, pltpu.roll(k0, lanes - 1, 1)),
                pltpu.roll(h0, lanes - 1, 1),
                pltpu.roll(c0, lanes - 1, 1),
            )
            fh, fs = face(here, right, False)
            hs, cs = fh - pltpu.roll(fh, 1, 1), fs - pltpu.roll(fs, 1, 1)
            if row_face is not None:
                hs, cs = hs - row_face[0], cs - row_face[1]
            if r < width - 1:
                row_face = face(
                    here, (k_ref[l, r + 1], x_ref[1, l, r + 1], x_ref[2, l, r + 1]), False
                )
                hs, cs = hs + row_face[0], cs + row_face[1]
            if l > 0:
                hs, cs = hs - lay_ref[0, r], cs - lay_ref[1, r]
            if l < layers - 1:
                fh, fs = face(here, (k_ref[l + 1, r], x_ref[1, l + 1, r], x_ref[2, l + 1, r]), True)
                lay_ref[0, r] = fh
                lay_ref[1, r] = fs
                hs, cs = hs + fh, cs + fs
            flat = l * width + r
            put(fc_ref, per + flat, h0 + head_rate * hs)
            put(fc_ref, 2 * per + flat, c0 + cs)


def step_edges(x_ref, up_ref, dn_ref, fc_ref, k_ref, has_up, has_dn):
    fields, layers, width, members, lanes = x_ref.shape
    per = layers * width
    for l in range(layers):
        for r, halo, has, sign in ((0, up_ref, has_up, -1.0), (width - 1, dn_ref, has_dn, 1.0)):
            here = (k_ref[l, r], x_ref[1, l, r], x_ref[2, l, r])
            there = (jnp.exp(halo[0, l]) * has, halo[1, l], halo[2, l])
            fh, fs = face(here, there, False) if sign > 0 else face(there, here, False)
            flat = l * width + r
            put(fc_ref, per + flat, get(fc_ref, per + flat) + (sign * head_rate) * fh)
            put(fc_ref, 2 * per + flat, get(fc_ref, 2 * per + flat) + sign * fs)


def observe(fc_ref, row_ref, hot_ref, pred_ref, per):
    groups = row_ref.shape[0]
    nm, members, lanes = fc_ref.shape[1:]
    first = per // nm
    rows = [jnp.broadcast_to(row_ref[g], (members, lanes)) for g in range(groups)]
    for g0 in range(0, groups, 8):
        part = range(g0, min(g0 + 8, groups))
        hot = hot_ref[:, g0 * lanes : (part[-1] + 1) * lanes]
        acc = [jnp.zeros((members, lanes), jnp.float32) for _ in part]
        for j in range(2 * per // nm):
            v = fc_ref[first + j].reshape(nm * members, lanes)
            hi = v.astype(jnp.bfloat16)
            left = v - hi.astype(jnp.float32)
            mid = left.astype(jnp.bfloat16)
            low = (left - mid.astype(jnp.float32)).astype(jnp.bfloat16)
            picked = jnp.dot(
                jnp.concatenate([hi, mid, low], axis=1), hot, preferred_element_type=jnp.float32
            )
            for q in range(nm):
                block = picked[q * members : (q + 1) * members]
                for i, g in enumerate(part):
                    acc[i] = jnp.where(
                        rows[g] == j * nm + q, block[:, i * lanes : (i + 1) * lanes], acc[i]
                    )
        for i, g in enumerate(part):
            pred_ref[g] = acc[i]


def analysis_kernel(
    x_in, row_ref, col_ref, noise_in, obs_ref, var_ref, out_ref,
    x_ref, noise_ref, hot_ref, fc_ref, pred_ref, k_ref, lay_ref, up_ref, dn_ref, pbuf, nbuf, part, rsbuf, gc, gbuf, obuf, sref, cref,
    s_pred, r_pred, s_noise, r_noise, s_fwd, r_fwd, s_rs, r_rs, s_ag, r_ag, s_back, r_back, s_loc, s_up, r_up, s_dn, r_dn,
):
    nm, nt = lax.axis_size("mem"), lax.axis_size("tile")
    n = nm * nt
    d, t = lax.axis_index("mem"), lax.axis_index("tile")
    me = d * nt + t
    gpc, members, lanes = pbuf.shape[2:]
    ncl = nm // nt
    total = nm * members
    reducers, blk, blk_lanes = gc.shape
    crows = gbuf.shape[0]
    worker = t == d // ncl

    def remote(src, dst, ss, rs, mem, tile):
        return pltpu.make_async_remote_copy(
            src_ref=src, dst_ref=dst, send_sem=ss, recv_sem=rs,
            device_id={"mem": mem, "tile": tile}, device_id_type=MESH,
        )

    def drain(ref, sem):
        pltpu.make_async_copy(ref, ref, sem).wait()

    barrier = pltpu.get_barrier_semaphore()

    def greet(i, _):
        to = lax.rem(me + i, n)
        pl.semaphore_signal(
            barrier, 1, device_id={"mem": to // nt, "tile": lax.rem(to, nt)}, device_id_type=MESH
        )
        return 0

    lax.fori_loop(1, n, greet, 0)
    fields, layers, width = x_ref.shape[:3]
    per = layers * width
    rows_all = fields * per
    for f in range(fields):
        for l in range(layers):
            for r in range(width):
                flat = f * per + l * width + r
                value = x_in[pl.ds(flat, members, stride=rows_all), :]
                x_ref[f, l, r] = value
                if f == 0:
                    put(fc_ref, flat, value)
    for g in range(noise_ref.shape[0]):
        noise_ref[g] = noise_in[pl.ds(g * lanes, lanes), :].T
    lane_of = lax.broadcasted_iota(jnp.int32, (lanes, lanes), 0)
    for g in range(col_ref.shape[0]):
        hot = jnp.where(lane_of == col_ref[g], 1.0, 0.0).astype(jnp.bfloat16)
        for piece in range(3):
            hot_ref[pl.ds(piece * lanes, lanes), pl.ds(g * lanes, lanes)] = hot
    step_inside(x_ref, fc_ref, k_ref, lay_ref)
    pl.semaphore_wait(barrier, n - 1)

    to_up = remote(x_ref.at[:, :, 0], dn_ref, s_up, r_up, d, jnp.maximum(t - 1, 0))
    to_dn = remote(x_ref.at[:, :, width - 1], up_ref, s_dn, r_dn, d, jnp.minimum(t + 1, nt - 1))

    @pl.when(t > 0)
    def _():
        to_up.start()

    @pl.when(t < nt - 1)
    def _():
        to_dn.start()

    mine = pl.ds(pl.multiple_of(d * members, members), members)

    def forward(first, end):
        for k in range(1, nm):
            c = lax.rem(d + k, nm)
            span = pl.ds(first, end - first)
            remote(fc_ref.at[span, c], gbuf.at[span, mine, :], s_fwd, r_fwd, c, t).start()

    @pl.when(t > 0)
    def _():
        to_dn.wait_recv()

    @pl.when(t == 0)
    def _():
        up_ref[...] = jnp.zeros_like(up_ref)

    @pl.when(t < nt - 1)
    def _():
        to_up.wait_recv()

    @pl.when(t == nt - 1)
    def _():
        dn_ref[...] = jnp.zeros_like(dn_ref)

    step_edges(
        x_ref, up_ref, dn_ref, fc_ref, k_ref,
        jnp.where(t > 0, 1.0, 0.0).astype(jnp.float32),
        jnp.where(t < nt - 1, 1.0, 0.0).astype(jnp.float32),
    )
    observe(fc_ref, row_ref, hot_ref, pred_ref, per)

    for k in range(nm):
        c = lax.rem(d + k, nm)
        src = pred_ref.at[pl.ds(c * gpc, gpc)]
        if k == 0:
            @pl.when(worker)
            def _():
                pbuf[t, d] = pred_ref[pl.ds(d * gpc, gpc)]

            @pl.when(jnp.logical_not(worker))
            def _():
                remote(src, pbuf.at[t, d], s_pred, r_pred, c, c // ncl).start()
        else:
            remote(src, pbuf.at[t, d], s_pred, r_pred, c, c // ncl).start()
    for j in range(ncl):
        c = t * ncl + j
        src = noise_ref.at[pl.ds(j * gpc, gpc)]

        @pl.when(c != d)
        def _():
            remote(src, nbuf.at[d], s_noise, r_noise, c, t).start()

        @pl.when(c == d)
        def _():
            nbuf[d] = noise_ref[pl.ds(j * gpc, gpc)]

    early = max(1, crows // 4)
    forward(0, early)

    @pl.when(worker)
    def _():
        drain(pbuf_flat(pbuf, n - 1), r_pred)
        drain(nbuf.at[pl.ds(0, nm - 1)], r_noise)
        gram = jnp.zeros((total, total), jnp.float32)
        cross = jnp.zeros((total, total), jnp.float32)
        base = lax.rem(d, ncl) * gpc
        for g in range(gpc):
            pred = pbuf[0, :, g]
            for q in range(1, nt):
                pred = pred + pbuf[q, :, g]
            pred = pred.reshape(total, lanes)
            noise = nbuf[:, g].reshape(total, lanes)
            scale = jnp.sqrt(alpha_mda * var_ref[base + g])
            innov = (obs_ref[base + g] - pred) / scale + noise
            anom = (pred - jnp.mean(pred, axis=0, keepdims=True)) / (
                scale * math.sqrt(total - 1)
            )
            dims = (((1,), (1,)), ((), ()))
            gram = gram + lax.dot_general(
                anom, anom, dims, precision=HI, preferred_element_type=jnp.float32
            )
            cross = cross + lax.dot_general(
                anom, innov, dims, precision=HI, preferred_element_type=jnp.float32
            )
        half = reducers // 2
        part[pl.ds(0, half)] = gram.reshape(half, blk, blk_lanes)
        part[pl.ds(half, half)] = cross.reshape(half, blk, blk_lanes)

        def scatter(i, _):
            to = lax.rem(me + i, n)

            @pl.when(to < reducers)
            def _():
                remote(part.at[to], rsbuf.at[d], s_rs, r_rs, to // nt, lax.rem(to, nt)).start()
            return 0

        lax.fori_loop(1, n, scatter, 0)

        @pl.when(me < reducers)
        def _():
            rsbuf[d] = part[me]

    @pl.when(me < reducers)
    def _():
        @pl.when(worker)
        def _():
            drain(rsbuf.at[pl.ds(0, nm - 1)], r_rs)

        @pl.when(jnp.logical_not(worker))
        def _():
            drain(rsbuf, r_rs)
        acc = rsbuf[0]
        for q in range(1, nm):
            acc = acc + rsbuf[q]
        gc[me] = acc

        def spread(i, _):
            to = lax.rem(me + i, n)
            remote(gc.at[me], gc.at[me], s_ag, r_ag, to // nt, lax.rem(to, nt)).start()
            return 0

        lax.fori_loop(1, n, spread, 0)

    forward(early, crows)
    local = pltpu.make_async_copy(fc_ref.at[:, d], gbuf.at[:, mine, :], s_loc)
    local.start()

    @pl.when(me < reducers)
    def _():
        drain(gc.at[pl.ds(0, reducers - 1)], r_ag)

    if reducers < n:
        @pl.when(me >= reducers)
        def _():
            drain(gc, r_ag)

    half = reducers // 2
    eye = (
        lax.broadcasted_iota(jnp.int32, (total, total), 0)
        == lax.broadcasted_iota(jnp.int32, (total, total), 1)
    ).astype(jnp.float32)
    sref[...] = gc[pl.ds(0, half)].reshape(total, total) + eye
    cref[...] = gc[pl.ds(half, half)].reshape(total, total)
    b = 16
    blane = lax.broadcasted_iota(jnp.int32, (b, total), 1)
    brow = lax.broadcasted_iota(jnp.int32, (b, total), 0)
    flane = lax.broadcasted_iota(jnp.int32, (total, total), 1)

    def sweep(g, _):
        first = pl.multiple_of(g * b, b)
        rows = sref[pl.ds(first, b), :]
        z_c = cref[pl.ds(first, b), :]
        piv = pltpu.roll(rows, lax.rem(total - first, total), 1)
        own = (blane >= first) & (blane < first + b)
        z_s = jnp.where(own, jnp.where(blane == brow + first, -1.0, 0.0), rows)
        for k in range(0, b, 2):
            c0 = jnp.broadcast_to(piv[:, k : k + 1], (b, total))
            c1 = jnp.broadcast_to(piv[:, k + 1 : k + 2], (b, total))
            p00, p10 = c0[k : k + 1], c0[k + 1 : k + 2]
            p01, p11 = c1[k : k + 1], c1[k + 1 : k + 2]
            inv = 1.0 / (p00 * p11 - p01 * p10)
            pair = (brow == k) | (brow == k + 1)
            f0, f1 = jnp.where(pair, 0.0, c0), jnp.where(pair, 0.0, c1)

            def upd(z):
                z0, z1 = z[k : k + 1] * inv, z[k + 1 : k + 2] * inv
                n0 = p11 * z0 - p01 * z1
                n1 = p00 * z1 - p10 * z0
                rest = z - f0 * n0 - f1 * n1
                return jnp.where(brow == k, n0, jnp.where(brow == k + 1, n1, rest))

            piv, z_s, z_c = upd(piv), upd(z_s), upd(z_c)
        left = rows.T
        keep = (flane >= first) & (flane < first + b)
        s_old = jnp.where(keep, 0.0, sref[...])
        s_new = s_old - jnp.dot(left, z_s, precision=HI, preferred_element_type=jnp.float32)
        c_new = cref[...] - jnp.dot(left, z_c, precision=HI, preferred_element_type=jnp.float32)
        sref[...] = s_new
        cref[...] = c_new
        sref[pl.ds(first, b), :] = z_s
        cref[pl.ds(first, b), :] = z_c
        return 0

    lax.fori_loop(0, total // b, sweep, 0)
    scaled = cref[...] / math.sqrt(total - 1)
    mix = (eye + scaled - jnp.mean(scaled, axis=0, keepdims=True)).T

    local.wait()
    drain(gbuf.at[:, pl.ds(0, (nm - 1) * members), :], r_fwd)
    parts = 3 if crows % 3 == 0 else 1
    pr = crows // parts
    for q in range(parts):
        for r in range(q * pr, (q + 1) * pr):
            obuf[r] = jnp.dot(mix, gbuf[r], precision=HI, preferred_element_type=jnp.float32)
        for k in range(1, nm):
            c = lax.rem(d + k, nm)
            theirs = pl.ds(pl.multiple_of(c * members, members), members)
            remote(
                obuf.at[pl.ds(q * pr, pr), theirs, :],
                out_ref.at[pl.ds(q * pr, pr), d],
                s_back, r_back, c, t,
            ).start()
    out_ref[:, d] = obuf[:, mine, :]

    @pl.when(t > 0)
    def _():
        to_up.wait_send()

    @pl.when(t < nt - 1)
    def _():
        to_dn.wait_send()

    @pl.when(worker)
    def _():
        drain(pred_ref.at[pl.ds(0, (nm - 1) * gpc)], s_pred)
        if reducers < n:
            @pl.when(me < reducers)
            def _():
                drain(part.at[pl.ds(0, reducers - 1)], s_rs)

            @pl.when(me >= reducers)
            def _():
                drain(part, s_rs)
        else:
            drain(part.at[pl.ds(0, reducers - 1)], s_rs)

    @pl.when(jnp.logical_not(worker))
    def _():
        drain(pred_ref, s_pred)

    @pl.when(worker)
    def _():
        if ncl > 1:
            drain(noise_ref.at[pl.ds(0, (ncl - 1) * gpc)], s_noise)

    @pl.when(jnp.logical_not(worker))
    def _():
        drain(noise_ref, s_noise)

    @pl.when(me < reducers)
    def _():
        def done(i, _):
            drain(gc.at[0], s_ag)
            return 0

        if reducers == n:
            drain(gc.at[pl.ds(0, n - 1)], s_ag)
        else:
            lax.fori_loop(1, n, done, 0)
    drain(fc_ref.at[:, pl.ds(0, nm - 1)], s_fwd)
    drain(obuf.at[:, pl.ds(0, (nm - 1) * members), :], s_back)
    drain(out_ref.at[:, pl.ds(0, nm - 1)], r_back)


def pbuf_flat(ref, count):
    nt, nm = ref.shape[:2]
    return ref.reshape((nt * nm,) + ref.shape[2:]).at[pl.ds(0, count)]


def local(fields_in, offsets, observed, obs_var, obs_noise):
    members, fields, layers, width, lanes = fields_in.shape
    rank = lax.axis_index("tile")
    nt, nm = lax.axis_size("tile"), lax.axis_size("mem")
    n = nt * nm
    rows = fields * layers * width
    x = fields_in.reshape(members * rows, lanes)
    plane = width * nt * lanes
    lay = offsets // plane
    rest = offsets % plane
    lrow = rest // lanes - rank * width
    row = jnp.where((lrow >= 0) & (lrow < width), lay * width + lrow, -1)
    groups = offsets.shape[0] // lanes
    row = row.reshape(groups, 1, lanes)
    col = (rest % lanes).reshape(groups, 1, lanes)
    f32 = jnp.float32
    gpc = groups // nm
    own = groups // nt
    obs = observed.reshape(own, 1, lanes)
    var = obs_var.reshape(own, 1, lanes)
    total = members * nm
    reducers = min(n, 2 * total // 8)
    blk = 2 * total // reducers
    crows = rows // nm
    dma = pltpu.SemaphoreType.DMA
    out = pl.pallas_call(
        analysis_kernel,
        out_shape=jax.ShapeDtypeStruct((crows, nm, members, lanes), f32),
        in_specs=[VM] * 6,
        out_specs=VM,
        scratch_shapes=[
            pltpu.VMEM((fields, layers, width, members, lanes), f32),
            pltpu.VMEM((own, members, lanes), f32),
            pltpu.VMEM((3 * lanes, groups * lanes), jnp.bfloat16),
            pltpu.VMEM((crows, nm, members, lanes), f32),
            pltpu.VMEM((groups, members, lanes), f32),
            pltpu.VMEM((layers, width, members, lanes), f32),
            pltpu.VMEM((2, width, members, lanes), f32),
            pltpu.VMEM((fields, layers, members, lanes), f32),
            pltpu.VMEM((fields, layers, members, lanes), f32),
            pltpu.VMEM((nt, nm, gpc, members, lanes), f32),
            pltpu.VMEM((nm, gpc, members, lanes), f32),
            pltpu.VMEM((reducers, blk, total), f32),
            pltpu.VMEM((nm, blk, total), f32),
            pltpu.VMEM((reducers, blk, total), f32),
            pltpu.VMEM((crows, total, lanes), f32),
            pltpu.VMEM((crows, total, lanes), f32),
            pltpu.VMEM((total, total), f32),
            pltpu.VMEM((total, total), f32),
        ]
        + [dma] * 17,
        compiler_params=pltpu.CompilerParams(collective_id=0, has_side_effects=True),
    )(x, row, col, obs_noise, obs, var)
    return out.reshape(fields, layers, width, members, lanes).transpose(3, 0, 1, 2, 4)


def solution(mesh):
    in_specs = (P("mem", None, None, "tile", None), P(), P("tile"), P("tile"), P("tile", "mem"))
    out_specs = P("mem", None, None, "tile", None)
    return jax.shard_map(local, mesh=mesh, in_specs=in_specs, out_specs=out_specs, check_vma=False)
```
